256 devices in a mesh: depth: 16 (over z, core), rows: 4 (over x), cols: 4 (over y).
Axes of the slice: x: 4, y: 4, z: 8, core: 2. Of those that a mesh axis runs over, the one named last changes fastest.
Arguments:
- section_states: float32 [16, 128, 64, 256], P('depth', 'rows', 'cols'), may hold values from -6 to 6
- weights: bfloat16 [32, 3, 3, 256, 256], P('depth'), may hold values from -0.125 to 0.125
Outputs:
- fine_states: float32 [32, 128, 64, 256], P('depth', 'rows', 'cols')
- coarse_states: float32 [16, 128, 64, 256], P('depth', 'rows', 'cols')
The draws below stay inside these ranges and needn't reach their ends.
All inputs are finite; a program needn't handle non-finite values.
Results may differ from the reference program's by a relative error of at most 0.002.
Values may be sent and summed in bfloat16 or wider, within the bound.
No kernel may reach another device: no remote copies, remote signals or barrier semaphores. Data moves between devices by JAX's collectives and lax.ppermute only.
A program may use at most 64 MiB of HBM per device.

```python
import jax
import jax.numpy as jnp
from jax import lax

C = 256
SECTIONS = 16
LAYERS = 32
HEIGHT = 128
WIDTH = 64


def level_of(rng, extent, cuts, least, high):
    loudness, own = 1.0, jax.random.fold_in(rng, 6)
    for dim, blocks in cuts:
        steps = jnp.exp(jax.random.uniform(jax.random.fold_in(own, dim), (blocks,), jnp.float32, least / len(cuts), high / len(cuts)))
        loudness = loudness * jnp.repeat(steps, extent[dim] // blocks).reshape([-1 if axis == dim else 1 for axis in range(len(extent))])
    return loudness


def gaussian(rng, extent, scale, reach, shards=(), held_as=jnp.bfloat16):
    drawn = jax.random.normal(rng, extent, jnp.float32) * scale
    if len(shards) > 0:
        drawn = level_of(rng, extent, shards, -0.22, 0.18) * drawn
    return jnp.clip(drawn, min=-reach, max=reach).astype(held_as)


def setup_inputs(seed: int = 0) -> dict:
    splits = jax.random.split(jax.random.key(seed), 3)
    section_states = gaussian(splits[0], (SECTIONS, HEIGHT, WIDTH, C), 1.0, 6.0, ((0, 16), (1, 4), (2, 4)), jnp.float32)
    weights = gaussian(splits[1], (LAYERS, 3, 3, C, C), (9 * C) ** -0.5, 0.125, ((0, 16),))
    return dict(section_states=section_states, weights=weights)


def velocity(field, kernel):
    rows_here, cols_here, channels = field.shape
    rounded = lax.optimization_barrier(jax.nn.silu(field).astype(jnp.bfloat16)).astype(jnp.float32)
    padded = jnp.pad(rounded, ((1, 1), (1, 1), (0, 0)))
    summed = jnp.zeros((rows_here * cols_here, channels), jnp.float32)
    for shift_row in range(3):
        for shift_col in range(3):
            window = padded[shift_row:shift_row + rows_here, shift_col:shift_col + cols_here].reshape(-1, channels)
            summed = summed + jnp.dot(window, kernel[shift_row, shift_col].astype(jnp.float32), preferred_element_type=jnp.float32)
    return summed.reshape(rows_here, cols_here, channels)


def reference(section_states, weights):
    step_size = 2.0 / LAYERS
    sections = section_states.shape[0]
    jump_list = []
    for section in range(sections):
        anchor = section_states[section]
        first_slope = velocity(anchor, weights[2 * section])
        middle = anchor + step_size * first_slope
        ending = middle + step_size * velocity(middle, weights[2 * section + 1])
        jump_list.append(ending - (anchor + 2.0 * step_size * first_slope))
    coarse = [section_states[0]]
    for section in range(sections - 1):
        current = coarse[-1]
        coarse.append(current + 2.0 * step_size * velocity(current, weights[2 * section]) + jump_list[section])
    fine_list = []
    for section in range(sections):
        middle = coarse[section] + step_size * velocity(coarse[section], weights[2 * section])
        ending = middle + step_size * velocity(middle, weights[2 * section + 1])
        fine_list.append(middle)
        fine_list.append(ending)
    return jnp.stack(fine_list), jnp.stack(coarse)
```

```python
import functools

import jax
import jax.numpy as jnp
from jax import lax
from jax.experimental import pallas as pl
from jax.experimental.pallas import tpu as pltpu
from jax.sharding import PartitionSpec as P

AXES = ("depth", "rows", "cols")
HALO = 3
BF16 = jnp.bfloat16
F32 = jnp.float32


def silu(x):
    return x / (1.0 + jnp.exp(-x))


def fill(patch, row, x, valid):
    width, channels = x.shape
    act = jnp.where(valid, silu(x), 0.0)
    column = lax.broadcasted_iota(jnp.int32, (width, channels), 0)
    left = jnp.where(column == 0, 0.0, pltpu.roll(act, 1, 0))
    right = jnp.where(column == width - 1, 0.0, pltpu.roll(act, width - 1, 0))
    for tap, moved in enumerate((left, act, right)):
        patch[row, :, tap * channels : (tap + 1) * channels] = moved.astype(BF16)


def slope(patch, weight, rows):
    width, deep = patch.shape[1:]
    total = None
    for tap in range(3):
        part = jnp.dot(
            patch[tap : tap + rows].reshape(rows * width, deep),
            weight[tap],
            preferred_element_type=F32,
        )
        total = part if total is None else total + part
    return total.reshape(rows, width, -1)


def in_image(strip, row, rows, height):
    place = strip * rows + row
    return (place >= 0) & (place < height)


def head_kernel(step, height, where, pieces, w0, w1, jump, main, top, bottom, strip, middle, patch, w0v, w1v, sems):
    rows = main.shape[0]
    deep = strip.shape[0]
    halo = (deep - rows) // 2
    wide = pieces.shape[2]
    index = where[1]
    loads = [pltpu.make_async_copy(w0, w0v, sems.at[0]), pltpu.make_async_copy(w1, w1v, sems.at[1])]
    loads += [
        pltpu.make_async_copy(pieces.at[k], strip.at[:, pl.ds(k * wide, wide), :], sems.at[2 + k])
        for k in range(pieces.shape[0])
    ]
    for load in loads:
        load.start()
    for load in loads[2:]:
        load.wait()
    main[...] = strip[halo : halo + rows]
    top[...] = strip[halo - HALO : halo].astype(BF16)
    bottom[...] = strip[halo + rows : halo + rows + HALO].astype(BF16)
    for row in range(deep):
        fill(patch, row, strip[row], in_image(index, row - halo, rows, height))
    loads[0].wait()
    first = slope(patch, w0v, deep - 2)
    jump[...] = -step * first[1 : deep - 3]
    middle[...] = strip[1 : deep - 1] + step * first
    for row in range(deep - 2):
        fill(patch, row, middle[row], in_image(index, row + 1 - halo, rows, height))
    loads[1].wait()
    jump[...] += step * slope(patch, w1v, deep - 4)


def turn_kernel(
    turn, step, height, where, main, top, bottom, wa, wb, ja, jb, saved_in, second_in,
    out, out_top, out_bottom, saved, second, state, edge, patch, wav, wbv, jav, jbv, sems,
):
    @pl.when(where[0] == turn)
    def _():
        rows = main.shape[0]
        deep = rows + 2 * HALO
        index = where[1]
        loads = [
            pltpu.make_async_copy(main, state.at[pl.ds(HALO, rows)], sems.at[0]),
            pltpu.make_async_copy(top, edge.at[0], sems.at[1]),
            pltpu.make_async_copy(bottom, edge.at[1], sems.at[2]),
            pltpu.make_async_copy(wa, wav, sems.at[3]),
            pltpu.make_async_copy(ja, jav, sems.at[4]),
            pltpu.make_async_copy(wb, wbv, sems.at[5]),
            pltpu.make_async_copy(jb.at[pl.ds(2, rows)], jbv, sems.at[6]),
        ]
        for load in loads:
            load.start()
        for load in loads[:3]:
            load.wait()
        state[:HALO] = edge[0].astype(F32)
        state[HALO + rows :] = edge[1].astype(F32)
        keep = pltpu.make_async_copy(state.at[pl.ds(1, deep - 2)], saved, sems.at[0])
        keep.start()
        for row in range(deep):
            fill(patch, row, state[row], in_image(index, row - HALO, rows, height))
        loads[3].wait()
        loads[4].wait()
        jav[...] += state[1 : deep - 1] + (2.0 * step) * slope(patch, wav, deep - 2)
        keep_second = pltpu.make_async_copy(jav, second, sems.at[1])
        keep_second.start()
        for row in range(rows + 2):
            fill(patch, row, jav[row + 1], in_image(index, row - 1, rows, height))
        loads[5].wait()
        loads[6].wait()
        out[...] = jav[2 : 2 + rows] + (2.0 * step) * slope(patch, wbv, rows) + jbv[...]
        out_top[...] = out[:HALO].astype(BF16)
        out_bottom[...] = out[rows - HALO :].astype(BF16)
        keep.wait()
        keep_second.wait()


def tail_kernel(step, height, where, mine, other, w0, w1, pieces, state, middle, patch, w0v, w1v, sems):
    rows = pieces.shape[2]
    deep = state.shape[0]
    wide = pieces.shape[3]
    index = where[1]
    loads = [pltpu.make_async_copy(w0, w0v, sems.at[0]), pltpu.make_async_copy(w1, w1v, sems.at[1])]
    for load in loads:
        load.start()
    held = pltpu.make_async_copy(mine, state, sems.at[2])
    sent = pltpu.make_async_copy(other, state, sems.at[2])

    @pl.when(where[2] == 0)
    def _():
        held.start()
        held.wait()

    @pl.when(where[2] != 0)
    def _():
        sent.start()
        sent.wait()

    for row in range(deep):
        fill(patch, row, state[row], in_image(index, row - 2, rows, height))
    loads[0].wait()
    middle[...] = state[1 : deep - 1] + step * slope(patch, w0v, deep - 2)
    for row in range(rows + 2):
        fill(patch, row, middle[row], in_image(index, row - 1, rows, height))
    loads[1].wait()
    ending = middle[1 : 1 + rows] + step * slope(patch, w1v, rows)
    for k in range(pieces.shape[0]):
        cut = slice(k * wide, (k + 1) * wide)
        pieces[k, 0] = state[2 : 2 + rows, cut]
        pieces[k, 1] = middle[1 : 1 + rows, cut]
        pieces[k, 2] = ending[:, cut]


def call(kernel, outs, scratch, inputs, in_vmem, out_vmem, aliases, vmem=60 << 20):
    place = {True: pltpu.VMEM, False: pl.ANY}
    return pl.pallas_call(
        kernel,
        out_shape=[jax.ShapeDtypeStruct(*o) for o in outs],
        in_specs=[pl.BlockSpec(memory_space=pltpu.SMEM)]
        + [pl.BlockSpec(memory_space=place[v]) for v in in_vmem],
        out_specs=[pl.BlockSpec(memory_space=place[v]) for v in out_vmem],
        scratch_shapes=scratch,
        input_output_aliases=aliases,
        compiler_params=pltpu.CompilerParams(vmem_limit_bytes=vmem),
    )(*inputs)


def swap_pieces(pieces, ncols):
    mine = lax.axis_index("cols")
    got = {}
    for shift in (2, 1, 3):
        given = lax.dynamic_index_in_dim(pieces, (mine + shift) % ncols, 0, keepdims=False)
        got[shift] = lax.ppermute(given, "cols", [(c, (c + shift) % ncols) for c in range(ncols)])
    got[0] = lax.dynamic_index_in_dim(pieces, mine, 0, keepdims=False)
    stacked = jnp.stack([got[0], got[1], got[2], got[3]])
    order = (mine - jnp.arange(ncols)) % ncols
    return jnp.stack([lax.dynamic_index_in_dim(stacked, order[k], 0, keepdims=False) for k in range(ncols)])


def on_device(section_states, weights):
    ndepth, nrows, ncols = (lax.axis_size(a) for a in AXES)
    depth, row, col = (lax.axis_index(a) for a in AXES)
    tile = section_states[0]
    tile_rows, tile_cols, channels = tile.shape
    height, width = tile_rows * nrows, tile_cols * ncols
    rows = tile_rows // ncols
    strips = nrows * ncols
    step = 2.0 / (2 * ndepth)
    where = jnp.stack([depth, row * ncols + col, depth % 2]).astype(jnp.int32)
    flat = weights.reshape(2, 3, 3 * channels, channels)
    w0, w1 = flat[0], flat[1]

    def route(src_depths, step_depth, step_strip):
        return [
            (d * strips + s, (d + step_depth) * strips + s + step_strip)
            for d in src_depths
            for s in range(strips)
            if 0 <= s + step_strip < strips
        ]

    even, odd = range(0, ndepth, 2), range(1, ndepth, 2)
    w_second = lax.ppermute(w0, AXES, route(odd, -1, 0))

    halo = HALO + 1
    up = [(i, i + 1) for i in range(nrows - 1)]
    down = [(j, i) for i, j in up]
    before = lax.ppermute(tile[tile_rows - halo :], "rows", up)
    after = lax.ppermute(tile[:halo], "rows", down)
    long = jnp.concatenate([before, tile, after], axis=0)
    pieces = jnp.stack([long[k * rows : k * rows + rows + 2 * halo] for k in range(ncols)])
    pieces = lax.all_to_all(pieces, "cols", 0, 0, tiled=True)

    deep = rows + 2 * halo
    strip = (rows, width, channels)
    edge = (HALO, width, channels)
    patch = lambda n: pltpu.VMEM((n, width, 3 * channels), BF16)
    wv = pltpu.VMEM((3, 3 * channels, channels), BF16)
    vm = lambda n: pltpu.VMEM((n, width, channels), F32)


    jump, main, top, bottom = call(
        functools.partial(head_kernel, step, height),
        [((deep - 4, width, channels), F32), (strip, F32), (edge, BF16), (edge, BF16)],
        [vm(deep), vm(deep - 2), patch(deep), wv, wv, pltpu.SemaphoreType.DMA((6,))],
        (where, pieces, w0, w1),
        (False,) * 3,
        (True,) * 4,
        {},
    )
    jump_second = lax.ppermute(jump, AXES, route(odd, -1, 0))
    long_strip = (rows + 4, width, channels)
    saved = jnp.zeros(long_strip, F32)
    second = jnp.zeros(long_strip, F32)
    for turn in range(0, ndepth, 2):
        out, out_top, out_bottom, saved, second = call(
            functools.partial(turn_kernel, turn, step, height),
            [(strip, F32), (edge, BF16), (edge, BF16), (long_strip, F32), (long_strip, F32)],
            [vm(rows + 2 * HALO), pltpu.VMEM((2, *edge), BF16), patch(rows + 2 * HALO), wv, wv, vm(rows + 4), vm(rows),
             pltpu.SemaphoreType.DMA((7,))],
            (where, main, top, bottom, w0, w_second, jump, jump_second, saved, second),
            (False,) * 9,
            (True, True, True, False, False),
            {8: 3, 9: 4},
        )
        if turn < ndepth - 2:
            main = lax.ppermute(out, AXES, route([turn], 2, 0))
            top = lax.ppermute(out_bottom, AXES, route([turn], 2, 1))
            bottom = lax.ppermute(out_top, AXES, route([turn], 2, -1))
    other = lax.ppermute(second, AXES, route(even, 1, 0))
    (pieces,) = call(
        functools.partial(tail_kernel, step, height),
        [((ncols, 3, rows, tile_cols, channels), F32)],
        [vm(rows + 4), vm(rows + 2), patch(rows + 4), wv, wv, pltpu.SemaphoreType.DMA((3,))],
        (where, saved, other, w0, w1),
        (False,) * 4,
        (True,),
        {},
    )
    whole = [
        lax.all_to_all(pieces[:, k], "cols", 0, 0, tiled=True).reshape(tile_rows, tile_cols, channels)
        for k in range(3)
    ]
    return jnp.stack(whole[1:]), whole[0][None]


def solution(mesh):
    in_specs = (P("depth", "rows", "cols", None), P("depth", None, None, None, None))
    out_specs = (P("depth", "rows", "cols", None), P("depth", "rows", "cols", None))
    return jax.shard_map(
        on_device, mesh=mesh, in_specs=in_specs, out_specs=out_specs, check_vma=False
    )
```

```python
import functools

import jax
import jax.numpy as jnp
from jax import lax
from jax.experimental import pallas as pl
from jax.experimental.pallas import tpu as pltpu
from jax.sharding import PartitionSpec as P

AXES = ("depth", "rows", "cols")
BF16 = jnp.bfloat16
F32 = jnp.float32
KEPT = 2
FIRST, LONG, LAST = 3, 5, 3


def fill(patch, state, rows, first, strip, height):
    width, channels = state.shape[1:]

    def body(row, carry):
        x = state[row]
        place = strip + first + row
        act = x / (1.0 + jnp.exp(-x))
        act = jnp.where((place >= 0) & (place < height), act, 0.0)
        column = lax.broadcasted_iota(jnp.int32, (width, channels), 0)
        left = jnp.where(column == 0, 0.0, pltpu.roll(act, 1, 0))
        right = jnp.where(column == width - 1, 0.0, pltpu.roll(act, width - 1, 0))
        for tap, moved in enumerate((left, act, right)):
            patch[row, :, tap * channels : (tap + 1) * channels] = moved.astype(BF16)
        return carry

    lax.fori_loop(*rows, body, 0)


def slope(patch, weight, first, rows):
    width, deep = patch.shape[1:]
    total = None
    for tap in range(3):
        part = jnp.dot(
            patch[first + tap : first + tap + rows].reshape(rows * width, deep),
            weight[tap],
            preferred_element_type=F32,
        )
        total = part if total is None else total + part
    return total.reshape(rows, width, -1)


def head_kernel(step, height, where, pieces, above, below, w0, w1, main, top, bottom, *rest):
    jumps, (state, middle, patch) = rest[:-3], rest[-3:]
    ncols, rows, wide = pieces.shape[:3]
    halo = above.shape[1]
    deep = rows + 2 * halo
    strip = where[1] * rows
    for k in range(ncols):
        cut = slice(k * wide, (k + 1) * wide)
        state[:halo, cut] = above[k].astype(F32)
        state[halo : halo + rows, cut] = pieces[k]
        state[halo + rows :, cut] = below[k].astype(F32)
    main[...] = state[halo : halo + rows]
    top[...] = state[halo - FIRST : halo].astype(BF16)
    bottom[...] = state[halo + rows : halo + rows + FIRST].astype(BF16)
    fill(patch, state, (0, deep), -halo, strip, height)
    first = slope(patch, w0, 0, deep - 2)
    middle[...] = state[1 : deep - 1] + step * first
    state[1 : deep - 1] = first
    fill(patch, middle, (0, deep - 2), 1 - halo, strip, height)
    jump = step * (slope(patch, w1, 0, deep - 4) - state[2 : deep - 2])
    for ref in jumps:
        cut = (deep - 4 - ref.shape[0]) // 2
        ref[...] = jump[cut : deep - 4 - cut]


def turn_kernel(host, count, last, given, step, height, where, main, top, bottom, *rest):
    weights, jumps = rest[:count], rest[count : 2 * count]
    rest = rest[2 * count + given :]
    kept = count + 1 if last else count
    if not last:
        out, out_top, out_bottom = rest[:3]
        rest = rest[3:]
    saved, (even, odd, patch, sems) = rest[:kept], rest[kept:]

    @pl.when(where[0] == host)
    def _():
        rows, width, channels = main.shape
        halo = top.shape[0]
        strip = where[1] * rows
        states = (even, odd)
        even[:halo] = top[...].astype(F32)
        even[halo : halo + rows] = main[...]
        even[halo + rows :] = bottom[...].astype(F32)
        keep = []
        for k in range(count + 1):
            here, there = states[k % 2], states[(k + 1) % 2]
            near = halo - k
            if k < kept:
                copy = pltpu.make_async_copy(here.at[pl.ds(halo - KEPT, rows + 2 * KEPT)], saved[k], sems.at[k])
                copy.start()
                keep.append(copy)
            if k == count:
                break
            far = near - 1 if k < count - 1 or last else 0
            fill(patch, here, (halo - far - 1, halo + rows + far + 1), -halo, strip, height)
            change = (2.0 * step) * slope(patch, weights[k], halo - far - 1, rows + 2 * far)
            cut = (jumps[k].shape[0] - rows) // 2 - far
            new = here[halo - far : halo + rows + far] + change + jumps[k][cut : cut + rows + 2 * far]
            if k == count - 1 and not last:
                edge = out_top.shape[0]
                out[...] = new
                out_top[...] = new[:edge].astype(BF16)
                out_bottom[...] = new[rows - edge :].astype(BF16)
                break
            if k >= 1:
                keep[k - 1].wait()
            there[halo - far : halo + rows + far] = new
        for copy in keep[max(count - 1, 0) if last else max(count - 2, 0) :]:
            copy.wait()


def tail_kernel(step, height, where, held, one, two, three, w0, w1, coarse, fine, state, middle, patch, sem):
    ncols, rows, wide = coarse.shape[:3]
    deep = state.shape[0]
    strip = where[1] * rows
    for k, source in enumerate((held, one, two, three)):

        @pl.when(where[2] == k)
        def _():
            copy = pltpu.make_async_copy(source, state, sem.at[0])
            copy.start()
            copy.wait()

    fill(patch, state, (0, deep), -KEPT, strip, height)
    middle[...] = state[1 : deep - 1] + step * slope(patch, w0, 0, deep - 2)
    fill(patch, middle, (0, deep - 2), 1 - KEPT, strip, height)
    ending = middle[1 : 1 + rows] + step * slope(patch, w1, 0, rows)
    for k in range(ncols):
        cut = slice(k * wide, (k + 1) * wide)
        coarse[k] = state[KEPT : KEPT + rows, cut]
        fine[k, 0] = middle[1 : 1 + rows, cut]
        fine[k, 1] = ending[:, cut]


def call(kernel, outs, scratch, inputs, vmem_in, vmem_out, aliases, work, vmem=24 << 20):
    place = {True: pltpu.VMEM, False: pl.ANY}
    return pl.pallas_call(
        kernel,
        out_shape=[jax.ShapeDtypeStruct(*o) for o in outs],
        in_specs=[pl.BlockSpec(memory_space=pltpu.SMEM)]
        + [pl.BlockSpec(memory_space=place[v]) for v in vmem_in],
        out_specs=[pl.BlockSpec(memory_space=place[v]) for v in vmem_out],
        scratch_shapes=scratch,
        input_output_aliases=aliases,
        compiler_params=pltpu.CompilerParams(vmem_limit_bytes=vmem),
        cost_estimate=pl.CostEstimate(flops=work, bytes_accessed=1 << 20, transcendentals=0),
    )(*inputs)


def on_device(section_states, weights):
    ndepth, nrows, ncols = (lax.axis_size(a) for a in AXES)
    depth, row, col = (lax.axis_index(a) for a in AXES)
    tile = section_states[0]
    tile_rows, tile_cols, channels = tile.shape
    height, width = tile_rows * nrows, tile_cols * ncols
    rows = tile_rows // ncols
    strips = nrows * ncols
    step = 2.0 / (2 * ndepth)
    flat = weights.reshape(2, 3, 3 * channels, channels)
    w0, w1 = flat[0], flat[1]

    hosts = [0, *range(2, ndepth - 2, 4), ndepth - 2]
    counts = [2] + [4] * (len(hosts) - 2) + [1]
    halos = [FIRST] + [LONG] * (len(hosts) - 2) + [LAST]
    owner = {h + k: k for h, n in zip(hosts, counts) for k in range(n + (n == 1))}
    role = jnp.array([owner[d] for d in range(ndepth)], jnp.int32)[depth]
    where = jnp.stack([depth, row * ncols + col, role]).astype(jnp.int32)

    def route(pairs, shift):
        return [
            (a * strips + s, b * strips + (s + shift))
            for a, b in pairs
            for s in range(strips)
            if 0 <= s + shift < strips
        ]

    def fetch(x, k):
        return lax.ppermute(x, AXES, route([(h + k, h) for h, n in zip(hosts, counts) if n > k], 0))

    def ring(x, shift):
        return lax.ppermute(x, ("rows", "cols"), [(s, (s + shift) % strips) for s in range(strips)])

    pieces = lax.all_to_all(tile.reshape(ncols, rows, tile_cols, channels), "cols", 0, 0, tiled=True)
    near = LONG + 1
    above = ring(pieces[:, rows - near :].astype(BF16), 1)
    below = ring(pieces[:, :near].astype(BF16), -1)
    all_weights = [w0] + [fetch(w0, k) for k in (1, 2, 3)]
    like = lambda n, t=F32: ((n, width, channels), t)
    vm = lambda n: pltpu.VMEM((n, width, channels), F32)
    patch = lambda n: pltpu.VMEM((n, width, 3 * channels), BF16)
    macs = 2 * 9 * channels * channels * width
    deep = rows + 2 * near
    spans = [rows + 2 * (near - 2), rows + 2 * (near - 3), rows + 2 * (near - 4), rows]
    main, top, bottom, *jumps = call(
        functools.partial(head_kernel, step, height),
        [like(rows), like(FIRST, BF16), like(FIRST, BF16)] + [like(n) for n in spans],
        [vm(deep), vm(deep - 2), patch(deep)],
        (where, pieces, above, below, w0, w1),
        (True,) * 5,
        (True,) * 7,
        {},
        macs * (2 * deep - 6),
    )
    all_jumps = [jumps[0]] + [fetch(jumps[k], k) for k in (1, 2, 3)]

    saved = []
    for turn, (host, count, halo) in enumerate(zip(hosts, counts, halos)):
        last = turn == len(hosts) - 1
        kept = count + 1 if last else count
        given = min(len(saved), kept)
        outs = [] if last else [like(rows), like(halos[turn + 1], BF16), like(halos[turn + 1], BF16)]
        inputs = (where, main, top, bottom, *all_weights[:count], *all_jumps[:count], *saved[:given])
        results = call(
            functools.partial(turn_kernel, host, count, last, given, step, height),
            outs + [like(rows + 2 * KEPT)] * kept,
            [vm(rows + 2 * halo), vm(rows + 2 * halo), patch(rows + 2 * halo), pltpu.SemaphoreType.DMA((5,))],
            inputs,
            (True,) * (3 + 2 * count) + (False,) * given,
            (True,) * len(outs) + (False,) * kept,
            {len(inputs) - given + k: len(outs) + k for k in range(given)},
            macs * 11 * count,
        )
        saved[:kept] = results[len(outs) :]
        if not last:
            pair = [(host, hosts[turn + 1])]
            main = lax.ppermute(results[0], AXES, route(pair, 0))
            top = lax.ppermute(results[2], AXES, route(pair, 1))
            bottom = lax.ppermute(results[1], AXES, route(pair, -1))

    def give(k):
        sized = [n + (n == 1) for n in counts]
        return lax.ppermute(saved[k], AXES, route([(h, h + k) for h, n in zip(hosts, sized) if n > k], 0))

    coarse, fine = call(
        functools.partial(tail_kernel, step, height),
        [((ncols, rows, tile_cols, channels), F32), ((ncols, 2, rows, tile_cols, channels), F32)],
        [vm(rows + 4), vm(rows + 2), patch(rows + 4), pltpu.SemaphoreType.DMA((1,))],
        (where, saved[0], give(1), give(2), give(3), w0, w1),
        (False,) * 4 + (True,) * 2,
        (True, True),
        {},
        macs * 18,
    )
    fine = lax.all_to_all(fine, "cols", 0, 0, tiled=True)
    coarse = lax.all_to_all(coarse, "cols", 0, 0, tiled=True)
    fine = fine.transpose(1, 0, 2, 3, 4).reshape(2, tile_rows, tile_cols, channels)
    return fine, coarse.reshape(1, tile_rows, tile_cols, channels)


def solution(mesh):
    in_specs = (P("depth", "rows", "cols", None), P("depth", None, None, None, None))
    out_specs = (P("depth", "rows", "cols", None), P("depth", "rows", "cols", None))
    return jax.shard_map(
        on_device, mesh=mesh, in_specs=in_specs, out_specs=out_specs, check_vma=False
    )
```

```python
import functools

import jax
import jax.numpy as jnp
from jax import lax
from jax.experimental import pallas as pl
from jax.experimental.pallas import tpu as pltpu
from jax.sharding import PartitionSpec as P

AXES = ("depth", "rows", "cols")
BF16 = jnp.bfloat16
F32 = jnp.float32
KEPT = 2
FIRST, LONG, LAST = 3, 5, 3


def fill(patch, state, rows, first, height, columns=None):
    width, channels = state.shape[1:]
    column = lax.broadcasted_iota(jnp.int32, (width, channels), 0)
    if columns is not None:
        place = columns[1] + jnp.where(column < width - 4, column, column - width)
        inside = (place >= 0) & (place < columns[0])

    def body(row, carry):
        x = state[row]
        act = x / (1.0 + jnp.exp(-x))
        act = jnp.where((first + row >= 0) & (first + row < height), act, 0.0)
        if columns is not None:
            act = jnp.where(inside, act, 0.0)
        left = pltpu.roll(act, 1, 0)
        right = pltpu.roll(act, width - 1, 0)
        if columns is None:
            left = jnp.where(column == 0, 0.0, left)
            right = jnp.where(column == width - 1, 0.0, right)
        for tap, moved in enumerate((left, act, right)):
            patch[row, :, tap * channels : (tap + 1) * channels] = moved.astype(BF16)
        return carry

    lax.fori_loop(*rows, body, 0)


def strip_row(rows):
    return (lax.axis_index("rows") * lax.axis_size("cols") + lax.axis_index("cols")) * rows


def slope(patch, weight, first, rows):
    width, deep = patch.shape[1:]
    total = None
    for tap in range(3):
        part = jnp.dot(
            patch[first + tap : first + tap + rows].reshape(rows * width, deep),
            weight[tap],
            preferred_element_type=F32,
        )
        total = part if total is None else total + part
    return total.reshape(rows, width, -1)


def head_kernel(step, height, pieces, above, below, w0, w1, main, top, bottom, *rest):
    jumps, (state, middle, patch) = rest[:-3], rest[-3:]
    ncols, rows, wide = pieces.shape[:3]
    halo = above.shape[1]
    deep = rows + 2 * halo
    strip = strip_row(rows)
    for k in range(ncols):
        cut = slice(k * wide, (k + 1) * wide)
        state[:halo, cut] = above[k].astype(F32)
        state[halo : halo + rows, cut] = pieces[k]
        state[halo + rows :, cut] = below[k].astype(F32)
    main[...] = state[halo : halo + rows]
    top[...] = state[halo - FIRST : halo].astype(BF16)
    bottom[...] = state[halo + rows : halo + rows + FIRST].astype(BF16)
    fill(patch, state, (0, deep), strip - halo, height)
    first = slope(patch, w0, 0, deep - 2)
    middle[...] = state[1 : deep - 1] + step * first
    state[1 : deep - 1] = first
    fill(patch, middle, (0, deep - 2), strip + 1 - halo, height)
    jump = step * (slope(patch, w1, 0, deep - 4) - state[2 : deep - 2])
    for ref in jumps:
        cut = (deep - 4 - ref.shape[0]) // 2
        ref[...] = jump[cut : deep - 4 - cut].astype(ref.dtype)


def turn_kernel(host, count, last, given, step, height, main, top, bottom, *rest):
    weights, jumps = rest[:count], rest[count : 2 * count]
    rest = rest[2 * count + given :]
    kept = count + 1 if last else count
    if not last:
        out, out_top, out_bottom = rest[:3]
        rest = rest[3:]
    saved, (state, patch) = rest[:kept], rest[kept:]

    @pl.when(lax.axis_index("depth") == host)
    def _():
        rows, width, channels = main.shape
        halo = top.shape[0]
        strip = strip_row(rows)
        state[:halo] = top[...].astype(F32)
        state[halo : halo + rows] = main[...]
        state[halo + rows :] = bottom[...].astype(F32)
        saved[0][...] = state[halo - KEPT : halo + rows + KEPT]
        for k in range(count):
            far = halo - k - 1 if k < count - 1 or last else 0
            fill(patch, state, (halo - far - 1, halo + rows + far + 1), strip - halo, height)
            change = (2.0 * step) * slope(patch, weights[k], halo - far - 1, rows + 2 * far)
            cut = (jumps[k].shape[0] - rows) // 2 - far
            jump = jumps[k][cut : cut + rows + 2 * far].astype(F32)
            new = state[halo - far : halo + rows + far] + change + jump
            if k < kept - 1:
                state[halo - far : halo + rows + far] = new
                saved[k + 1][...] = new[far - KEPT : far + rows + KEPT]
            else:
                edge = out_top.shape[0]
                out[...] = new
                out_top[...] = new[:edge].astype(BF16)
                out_bottom[...] = new[rows - edge :].astype(BF16)


def pack_kernel(held, one, two, three, packed, state):
    depth = lax.axis_index("depth")
    role = jnp.where(depth < 2, depth, (depth - 2) % 4)
    for k, source in enumerate((held, one, two, three)):

        @pl.when(role == k)
        def _():
            state[...] = source[...]

    ncols = packed.shape[0]
    deep, width, channels = state.shape
    wide = width // ncols
    rows = deep - 2 * KEPT
    first = lax.axis_index("cols") == 0
    group = lax.broadcasted_iota(jnp.int32, (8, channels), 0)
    span = wide + 8
    for k in range(ncols):
        for row in range(rows + KEPT):
            if row < rows:
                line = lambda a, b: state[KEPT + row, a:b]
            else:
                line = lambda a, b: jnp.where(first, state[row - rows, a:b], state[KEPT + row, a:b])
            mine = line(k * wide, (k + 1) * wide)
            right = line((k + 1) * wide, (k + 1) * wide + 8) if k < ncols - 1 else jnp.zeros((8, channels), F32)
            left = line(k * wide - 8, k * wide) if k > 0 else jnp.zeros((8, channels), F32)
            high = mine.astype(BF16)
            packed[k, row * span : row * span + wide] = high
            packed[k, row * span + wide : (row + 1) * span] = jnp.where(group < 4, right, left).astype(BF16)
            if row < rows:
                start = (rows + KEPT) * span + row * wide
                packed[k, start : start + wide] = (mine - high.astype(F32)).astype(BF16)


def tail_kernel(step, height, width, packed, w0, w1, fine, coarse, state, middle, patch):
    ncols = packed.shape[0]
    tile_rows, wide = coarse.shape[:2]
    rows = tile_rows // ncols
    span = wide + 8
    for k in range(ncols):
        for row in range(rows):
            start = (rows + KEPT) * span + row * wide
            high = packed[k, row * span : (row + 1) * span].astype(F32)
            whole = high[:wide] + packed[k, start : start + wide].astype(F32)
            place = k * rows + row
            coarse[place] = whole
            state[KEPT + place, :wide] = whole
            state[KEPT + place, wide:] = high[wide:]
    for row in range(KEPT):
        cut = slice((rows + row) * span, (rows + row + 1) * span)
        state[row] = packed[0, cut].astype(F32)
        state[KEPT + tile_rows + row] = packed[ncols - 1, cut].astype(F32)
    top = lax.axis_index("rows") * tile_rows
    columns = (width, lax.axis_index("cols") * wide)
    fill(patch, state, (0, tile_rows + 4), top - 2, height, columns)
    middle[...] = state[1 : tile_rows + 3] + step * slope(patch, w0, 0, tile_rows + 2)
    fill(patch, middle, (0, tile_rows + 2), top - 1, height, columns)
    fine[0] = middle[1 : tile_rows + 1, :wide]
    ending = step * slope(patch, w1, 0, tile_rows)
    fine[1] = middle[1 : tile_rows + 1, :wide] + ending[:, :wide]


def call(kernel, outs, scratch, inputs, aliases={}, vmem=16 << 20):
    return pl.pallas_call(
        kernel,
        out_shape=[jax.ShapeDtypeStruct(*o) for o in outs],
        in_specs=[pl.BlockSpec(memory_space=pltpu.VMEM)] * len(inputs),
        out_specs=[pl.BlockSpec(memory_space=pltpu.VMEM)] * len(outs),
        scratch_shapes=scratch,
        input_output_aliases=aliases,
        compiler_params=pltpu.CompilerParams(vmem_limit_bytes=vmem),
    )(*inputs)


def on_device(section_states, weights):
    ndepth, nrows, ncols = (lax.axis_size(a) for a in AXES)
    tile = section_states[0]
    tile_rows, tile_cols, channels = tile.shape
    height, width = tile_rows * nrows, tile_cols * ncols
    rows = tile_rows // ncols
    strips = nrows * ncols
    step = 2.0 / (2 * ndepth)
    flat = weights.reshape(2, 3, 3 * channels, channels)
    w0, w1 = flat[0], flat[1]

    hosts = [0, *range(2, ndepth - 2, 4), ndepth - 2]
    counts = [2] + [4] * (len(hosts) - 2) + [1]
    halos = [FIRST] + [LONG] * (len(hosts) - 2) + [LAST]
    def route(pairs, shift):
        return [
            (a * strips + s, b * strips + (s + shift))
            for a, b in pairs
            for s in range(strips)
            if 0 <= s + shift < strips
        ]

    def fetch(x, k):
        return lax.ppermute(x, AXES, route([(h + k, h) for h, n in zip(hosts, counts) if n > k], 0))

    def ring(x, shift):
        return lax.ppermute(x, ("rows", "cols"), [(s, (s + shift) % strips) for s in range(strips)])

    pieces = lax.all_to_all(tile.reshape(ncols, rows, tile_cols, channels), "cols", 0, 0, tiled=True)
    near = LONG + 1
    above = ring(pieces[:, rows - near :].astype(BF16), 1)
    below = ring(pieces[:, :near].astype(BF16), -1)
    all_weights = [w0] + [fetch(w0, k) for k in (1, 2, 3)]
    like = lambda n, t=F32: ((n, width, channels), t)
    vm = lambda n: pltpu.VMEM((n, width, channels), F32)
    patch = lambda n: pltpu.VMEM((n, width, 3 * channels), BF16)
    deep = rows + 2 * near
    spans = [rows + 2 * (near - 2), rows + 2 * (near - 3), rows + 2 * (near - 4), rows]
    kinds = [F32, F32, BF16, BF16]
    main, top, bottom, *jumps = call(
        functools.partial(head_kernel, step, height),
        [like(rows), like(FIRST, BF16), like(FIRST, BF16)] + [like(n, t) for n, t in zip(spans, kinds)],
        [vm(deep), vm(deep - 2), patch(deep)],
        (pieces, above, below, w0, w1),
    )
    *all_weights[2:], jumps[2], jumps[3] = lax.optimization_barrier((*all_weights[2:], jumps[2], jumps[3]))
    fetched = [fetch(jumps[k], k) for k in (1, 2, 3)]
    main, top, bottom, *fetched = lax.optimization_barrier((main, top, bottom, *fetched))
    all_jumps = [jumps[0], *fetched]

    saved = []
    for turn, (host, count, halo) in enumerate(zip(hosts, counts, halos)):
        last = turn == len(hosts) - 1
        kept = count + 1 if last else count
        given = min(len(saved), kept)
        outs = [] if last else [like(rows), like(halos[turn + 1], BF16), like(halos[turn + 1], BF16)]
        inputs = (main, top, bottom, *all_weights[:count], *all_jumps[:count], *saved[:given])
        results = call(
            functools.partial(turn_kernel, host, count, last, given, step, height),
            outs + [like(rows + 2 * KEPT)] * kept,
            [vm(rows + 2 * halo), patch(rows + 2 * halo)],
            inputs,
            {len(inputs) - given + k: len(outs) + k for k in range(given)},
        )
        saved[:kept] = results[len(outs) :]
        if not last:
            pair = [(host, hosts[turn + 1])]
            main = lax.ppermute(results[0], AXES, route(pair, 0))
            top = lax.ppermute(results[2], AXES, route(pair, 1))
            bottom = lax.ppermute(results[1], AXES, route(pair, -1))

    def give(k):
        sized = [n + (n == 1) for n in counts]
        return lax.ppermute(saved[k], AXES, route([(h, h + k) for h, n in zip(hosts, sized) if n > k], 0))

    span = tile_cols + 8
    pixels = (rows + KEPT) * span + rows * tile_cols
    (packed,) = call(
        pack_kernel,
        [((ncols, pixels, channels), BF16)],
        [vm(rows + 2 * KEPT)],
        (saved[0], give(1), give(2), give(3)),
    )
    packed = lax.all_to_all(packed, "cols", 0, 0, tiled=True)
    tall = lambda n, t=F32, taps=1: pltpu.VMEM((n, span, taps * channels), t)
    fine, coarse = call(
        functools.partial(tail_kernel, step, height, width),
        [((2, *tile.shape), F32), (tile.shape, F32)],
        [tall(tile_rows + 4), tall(tile_rows + 2), tall(tile_rows + 4, BF16, 3)],
        (packed, w0, w1),
    )
    return fine, coarse[None]


def solution(mesh):
    in_specs = (P("depth", "rows", "cols", None), P("depth", None, None, None, None))
    out_specs = (P("depth", "rows", "cols", None), P("depth", "rows", "cols", None))
    return jax.shard_map(
        on_device, mesh=mesh, in_specs=in_specs, out_specs=out_specs, check_vma=False
    )
```

```python
import functools

import jax
import jax.numpy as jnp
from jax import lax
from jax.experimental import pallas as pl
from jax.experimental.pallas import tpu as pltpu
from jax.sharding import PartitionSpec as P

AXES = ("depth", "rows", "cols")
BF16 = jnp.bfloat16
F32 = jnp.float32
KEPT = 2
SLOTS = {"prev": -1, "own": 0, "core": 1, "next": 2}
JUMP_HALO = {"prev": 4, "own": 3, "core": 2, "next": 0}


CHUNK = 2


def fill_row(patch, row, x, valid, inside=None):
    width, channels = x.shape
    act = x / (1.0 + jnp.exp(-x))
    act = jnp.where(valid, act, 0.0)
    if inside is not None:
        act = jnp.where(inside, act, 0.0)
    left = pltpu.roll(act, 1, 0)
    right = pltpu.roll(act, width - 1, 0)
    if inside is None:
        column = lax.broadcasted_iota(jnp.int32, (width, channels), 0)
        left = jnp.where(column == 0, 0.0, left)
        right = jnp.where(column == width - 1, 0.0, right)
    for tap, moved in enumerate((left, act, right)):
        patch[row, :, tap * channels : (tap + 1) * channels] = moved.astype(BF16)


def fill(patch, state, rows, first, height, inside=None):
    def body(row, carry):
        fill_row(patch, row, state[row], (first + row >= 0) & (first + row < height), inside)
        return carry

    lax.fori_loop(0, rows, body, 0, unroll=2)


def slopes(patch, weight, first, rows, emit, chunk=CHUNK):
    width, deep = patch.shape[1:]
    for start in range(first, first + rows, chunk):
        count = min(chunk, first + rows - start)
        total = None
        for tap in range(3):
            part = jnp.dot(
                patch[start + tap - 1 : start + tap - 1 + count].reshape(count * width, deep),
                weight[tap],
                preferred_element_type=F32,
            )
            total = part if total is None else total + part
        total = total.reshape(count, width, -1)
        for k in range(count):
            emit(start + k, total[k])


def strip_row(rows):
    return (lax.axis_index("rows") * lax.axis_size("cols") + lax.axis_index("cols")) * rows


def head_kernel(step, height, pieces, above, below, w0, w1, main, top, bottom, *rest):
    jumps, (state, first, patch, second) = rest[:-4], rest[-4:]
    ncols, rows, wide = pieces.shape[:3]
    halo = above.shape[1]
    deep = rows + 2 * halo
    origin = strip_row(rows) - halo
    for k in range(ncols):
        cut = slice(k * wide, (k + 1) * wide)
        state[:halo, cut] = above[k].astype(F32)
        state[halo : halo + rows, cut] = pieces[k]
        state[halo + rows :, cut] = below[k].astype(F32)
    main[...] = state[halo : halo + rows]
    top[...] = state[halo - top.shape[0] : halo].astype(BF16)
    bottom[...] = state[halo + rows : halo + rows + bottom.shape[0]].astype(BF16)
    fill(patch, state, deep, origin, height)

    def to_middle(row, slope):
        first[row] = slope
        valid = (origin + row >= 0) & (origin + row < height)
        fill_row(second, row, state[row] + step * slope, valid)

    def to_jump(row, slope):
        jump = step * (slope - first[row])
        for ref in jumps:
            place = row - (deep - ref.shape[0]) // 2
            if 0 <= place < ref.shape[0]:
                ref[place] = jump.astype(ref.dtype)

    slopes(patch, w0, 1, deep - 2, to_middle)
    slopes(second, w1, 2, deep - 4, to_jump)


def turn_kernel(host, count, kept, given, last, step, height, main, top, bottom, *rest):
    weights, jumps = rest[:count], rest[count : 2 * count]
    rest = rest[2 * count + given :]
    if not last:
        out, out_top, out_bottom = rest[:3]
        rest = rest[3:]
    saved, (state, *patches) = rest[:kept], rest[kept:]

    @pl.when(lax.axis_index("depth") == host)
    def _():
        rows, width, channels = main.shape
        halo = top.shape[0]
        origin = strip_row(rows) - halo
        state[:halo] = top[...].astype(F32)
        state[halo : halo + rows] = main[...]
        state[halo + rows :] = bottom[...].astype(F32)
        saved[0][...] = state[halo - KEPT : halo + rows + KEPT]
        fill(patches[0], state, rows + 2 * halo, origin, height)
        for k in range(count):
            ends = k == count - 1
            far = 0 if ends and not last else halo - k - 1
            cut = halo - (jumps[k].shape[0] - rows) // 2

            def advance(row, slope):
                new = state[row] + (2.0 * step) * slope + jumps[k][row - cut].astype(F32)
                if k < kept - 1 and halo - KEPT <= row < halo + rows + KEPT:
                    saved[k + 1][row - halo + KEPT] = new
                if not ends:
                    state[row] = new
                    fill_row(patches[(k + 1) % 2], row, new, (origin + row >= 0) & (origin + row < height))
                elif not last:
                    place, edge = row - halo, out_top.shape[0]
                    out[place] = new
                    if place < edge:
                        out_top[place] = new.astype(BF16)
                    if place >= rows - edge:
                        out_bottom[place - rows + edge] = new.astype(BF16)

            slopes(patches[k % 2], weights[k], halo - far, rows + 2 * far, advance)


def pack_kernel(own, core, after, prev, packed, state):
    depth = lax.axis_index("depth")
    final = 4 * ((lax.axis_size("depth") - 1) // 4) + 2
    role = jnp.where(depth < final, depth % 4, depth - final)
    for k, source in enumerate((own, core, after, prev)):

        @pl.when(role == k)
        def _():
            state[...] = source[...]

    ncols = packed.shape[0]
    deep, width, channels = state.shape
    wide = width // ncols
    rows = deep - 2 * KEPT
    first = lax.axis_index("cols") == 0
    group = lax.broadcasted_iota(jnp.int32, (8, channels), 0)
    span = wide + 8
    for k in range(ncols):
        for row in range(rows + KEPT):
            if row < rows:
                line = lambda a, b: state[KEPT + row, a:b]
            else:
                line = lambda a, b: jnp.where(first, state[row - rows, a:b], state[KEPT + row, a:b])
            mine = line(k * wide, (k + 1) * wide)
            right = line((k + 1) * wide, (k + 1) * wide + 8) if k < ncols - 1 else jnp.zeros((8, channels), F32)
            left = line(k * wide - 8, k * wide) if k > 0 else jnp.zeros((8, channels), F32)
            high = mine.astype(BF16)
            packed[k, row * span : row * span + wide] = high
            packed[k, row * span + wide : (row + 1) * span] = jnp.where(group < 4, right, left).astype(BF16)
            if row < rows:
                start = (rows + KEPT) * span + row * wide
                packed[k, start : start + wide] = (mine - high.astype(F32)).astype(BF16)


def tail_kernel(step, height, width, packed, w0, w1, fine, coarse, state, patch, second):
    ncols = packed.shape[0]
    tile_rows, wide = coarse.shape[:2]
    rows = tile_rows // ncols
    span = wide + 8
    for k in range(ncols):
        for row in range(rows):
            start = (rows + KEPT) * span + row * wide
            high = packed[k, row * span : (row + 1) * span].astype(F32)
            whole = high[:wide] + packed[k, start : start + wide].astype(F32)
            place = k * rows + row
            coarse[place] = whole
            state[KEPT + place, :wide] = whole
            state[KEPT + place, wide:] = high[wide:]
    for row in range(KEPT):
        cut = slice((rows + row) * span, (rows + row + 1) * span)
        state[row] = packed[0, cut].astype(F32)
        state[KEPT + tile_rows + row] = packed[ncols - 1, cut].astype(F32)
    top = lax.axis_index("rows") * tile_rows - KEPT
    column = lax.broadcasted_iota(jnp.int32, (span, state.shape[2]), 0)
    place = lax.axis_index("cols") * wide + jnp.where(column < span - 4, column, column - span)
    inside = (place >= 0) & (place < width)
    fill(patch, state, tile_rows + 2 * KEPT, top, height, inside)

    def to_middle(row, slope):
        middle = state[row] + step * slope
        if KEPT <= row < KEPT + tile_rows:
            fine[0, row - KEPT] = middle[:wide]
        fill_row(second, row, middle, (top + row >= 0) & (top + row < height), inside)

    def to_ending(row, slope):
        fine[1, row - KEPT] = fine[0, row - KEPT] + step * slope[:wide]

    slopes(patch, w0, 1, tile_rows + 2, to_middle, 2 * CHUNK)
    slopes(second, w1, 2, tile_rows, to_ending, 2 * CHUNK)


def call(kernel, outs, scratch, inputs, aliases={}, vmem=12 << 20):
    return pl.pallas_call(
        kernel,
        out_shape=[jax.ShapeDtypeStruct(*o) for o in outs],
        in_specs=[pl.BlockSpec(memory_space=pltpu.VMEM)] * len(inputs),
        out_specs=[pl.BlockSpec(memory_space=pltpu.VMEM)] * len(outs),
        scratch_shapes=scratch,
        input_output_aliases=aliases,
        compiler_params=pltpu.CompilerParams(vmem_limit_bytes=vmem),
    )(*inputs)


def on_device(section_states, weights):
    ndepth, nrows, ncols = (lax.axis_size(a) for a in AXES)
    tile = section_states[0]
    tile_rows, tile_cols, channels = tile.shape
    height, width = tile_rows * nrows, tile_cols * ncols
    rows = tile_rows // ncols
    strips = nrows * ncols
    step = 2.0 / (2 * ndepth)
    flat = weights.reshape(2, 3, 3 * channels, channels)
    w0, w1 = flat[0], flat[1]

    hosts = [*range(0, ndepth, 4), ndepth - 2]
    visits = [["own", "core", "next"]] + [["prev", "own", "core", "next"]] * (len(hosts) - 2) + [["own"]]
    visits[-2] = ["prev", "own", "core"]
    halos = [len(v) + 1 for v in visits]
    halos[-1] += 1

    def route(pairs, shift):
        return [
            (a * strips + s, b * strips + (s + shift))
            for a, b in pairs
            for s in range(strips)
            if 0 <= s + shift < strips
        ]

    def fetch(x, slot):
        away = SLOTS[slot]
        return lax.ppermute(x, AXES, route([(h + away, h) for h, v in zip(hosts, visits) if slot in v], 0))

    def ring(x, shift):
        return lax.ppermute(x, ("rows", "cols"), [(s, (s + shift) % strips) for s in range(strips)])

    pieces = lax.all_to_all(tile.reshape(ncols, rows, tile_cols, channels), "cols", 0, 0, tiled=True)
    near = JUMP_HALO["prev"] + 2
    above = ring(pieces[:, rows - near :].astype(BF16), 1)
    below = ring(pieces[:, :near].astype(BF16), -1)
    far = ("core", "next", "prev")
    all_weights = {"own": w0} | {slot: fetch(w0, slot) for slot in far}
    like = lambda n, t=F32: ((n, width, channels), t)
    vm = lambda n: pltpu.VMEM((n, width, channels), F32)
    patch = lambda n: pltpu.VMEM((n, width, 3 * channels), BF16)
    deep = rows + 2 * near
    kinds = {"prev": BF16, "own": F32, "core": F32, "next": BF16}
    main, top, bottom, *jumps = call(
        functools.partial(head_kernel, step, height),
        [like(rows), like(halos[0], BF16), like(halos[0], BF16)]
        + [like(rows + 2 * JUMP_HALO[slot], kinds[slot]) for slot in SLOTS],
        [vm(deep), vm(deep), patch(deep), patch(deep)],
        (pieces, above, below, w0, w1),
    )
    all_jumps = dict(zip(SLOTS, jumps))
    all_jumps |= {slot: fetch(all_jumps[slot], slot) for slot in far}
    main, top, bottom, all_weights["prev"] = lax.optimization_barrier((main, top, bottom, all_weights["prev"]))

    saved = {}
    for turn, (host, visit, halo) in enumerate(zip(hosts, visits, halos)):
        last = turn == len(hosts) - 1
        keeps = [*visit, "core"] if last else visit
        given = [slot for slot in keeps if slot in saved]
        outs = [] if last else [like(rows), like(halos[turn + 1], BF16), like(halos[turn + 1], BF16)]
        inputs = (
            main, top, bottom,
            *(all_weights[slot] for slot in visit),
            *(all_jumps[slot] for slot in visit),
            *(saved[slot] for slot in given),
        )
        results = call(
            functools.partial(turn_kernel, host, len(visit), len(keeps), len(given), last, step, height),
            outs + [like(rows + 2 * KEPT)] * len(keeps),
            [vm(rows + 2 * halo), patch(rows + 2 * halo), patch(rows + 2 * halo)],
            inputs,
            {len(inputs) - len(given) + k: len(outs) + keeps.index(slot) for k, slot in enumerate(given)},
        )
        saved |= zip(keeps, results[len(outs) :])
        if not last:
            pair = [(host, hosts[turn + 1])]
            main = lax.ppermute(results[0], AXES, route(pair, 0))
            top = lax.ppermute(results[2], AXES, route(pair, 1))
            bottom = lax.ppermute(results[1], AXES, route(pair, -1))

    visits[-1] = ["own", "core"]

    def give(slot):
        away = SLOTS[slot]
        return lax.ppermute(saved[slot], AXES, route([(h, h + away) for h, v in zip(hosts, visits) if slot in v], 0))

    span = tile_cols + 8
    pixels = (rows + KEPT) * span + rows * tile_cols
    (packed,) = call(
        pack_kernel,
        [((ncols, pixels, channels), BF16)],
        [vm(rows + 2 * KEPT)],
        (saved["own"], give("core"), give("next"), give("prev")),
    )
    packed = lax.all_to_all(packed, "cols", 0, 0, tiled=True)
    tall = lambda n, t=F32, taps=1: pltpu.VMEM((n, span, taps * channels), t)
    fine, coarse = call(
        functools.partial(tail_kernel, step, height, width),
        [((2, *tile.shape), F32), (tile.shape, F32)],
        [tall(tile_rows + 4), tall(tile_rows + 4, BF16, 3), tall(tile_rows + 4, BF16, 3)],
        (packed, w0, w1),
    )
    return fine, coarse[None]


def solution(mesh):
    in_specs = (P("depth", "rows", "cols", None), P("depth", None, None, None, None))
    out_specs = (P("depth", "rows", "cols", None), P("depth", "rows", "cols", None))
    return jax.shard_map(
        on_device, mesh=mesh, in_specs=in_specs, out_specs=out_specs, check_vma=False
    )
```

```python
import functools

import jax
import jax.numpy as jnp
from jax import lax
from jax.experimental import pallas as pl
from jax.experimental.pallas import tpu as pltpu
from jax.sharding import PartitionSpec as P

AXES = ("depth", "rows", "cols")
BF16 = jnp.bfloat16
F32 = jnp.float32
KEPT = 2
SLOTS = {"prev": -1, "own": 0, "core": 1, "next": 2}
JUMP_HALO = {"prev": 4, "own": 3, "core": 2, "next": 0}


CHUNK = 2


def fill_row(patch, row, x, valid, inside=None):
    width, channels = x.shape
    act = x / (1.0 + jnp.exp(-x))
    act = jnp.where(valid, act, 0.0)
    if inside is not None:
        act = jnp.where(inside, act, 0.0)
    left = pltpu.roll(act, 1, 0)
    right = pltpu.roll(act, width - 1, 0)
    if inside is None:
        column = lax.broadcasted_iota(jnp.int32, (width, channels), 0)
        left = jnp.where(column == 0, 0.0, left)
        right = jnp.where(column == width - 1, 0.0, right)
    for tap, moved in enumerate((left, act, right)):
        patch[row, :, tap * channels : (tap + 1) * channels] = moved.astype(BF16)


def fill(patch, state, rows, first, height, inside=None):
    def body(row, carry):
        fill_row(patch, row, state[row], (first + row >= 0) & (first + row < height), inside)
        return carry

    lax.fori_loop(0, rows, body, 0, unroll=2)


def slopes(patch, weight, first, rows, emit, chunk=CHUNK):
    width, deep = patch.shape[1:]
    for start in range(first, first + rows, chunk):
        count = min(chunk, first + rows - start)
        total = None
        for tap in range(3):
            part = jnp.dot(
                patch[start + tap - 1 : start + tap - 1 + count].reshape(count * width, deep),
                weight[tap],
                preferred_element_type=F32,
            )
            total = part if total is None else total + part
        total = total.reshape(count, width, -1)
        for k in range(count):
            emit(start + k, total[k])


def strip_row(rows):
    return (lax.axis_index("rows") * lax.axis_size("cols") + lax.axis_index("cols")) * rows


def hold_kernel(given, held):
    held[...] = given[...]


def edge_kernel(pieces, low, high):
    rows, count = pieces.shape[1], low.shape[1]
    low[...] = pieces[:, :count].astype(BF16)
    high[...] = pieces[:, rows - count :].astype(BF16)


def head_kernel(step, height, pieces, above, below, w0, w1, main, top, bottom, *rest):
    jumps, (state, first, patch, second) = rest[:-4], rest[-4:]
    ncols, rows, wide = pieces.shape[:3]
    halo = above.shape[1]
    deep = rows + 2 * halo
    origin = strip_row(rows) - halo
    for k in range(ncols):
        cut = slice(k * wide, (k + 1) * wide)
        state[:halo, cut] = above[k].astype(F32)
        state[halo : halo + rows, cut] = pieces[k]
        state[halo + rows :, cut] = below[k].astype(F32)
    main[...] = state[halo : halo + rows]
    top[...] = state[halo - top.shape[0] : halo].astype(BF16)
    bottom[...] = state[halo + rows : halo + rows + bottom.shape[0]].astype(BF16)
    fill(patch, state, deep, origin, height)

    def to_middle(row, slope):
        first[row] = slope
        valid = (origin + row >= 0) & (origin + row < height)
        fill_row(second, row, state[row] + step * slope, valid)

    def to_jump(row, slope):
        jump = step * (slope - first[row])
        for ref in jumps:
            place = row - (deep - ref.shape[0]) // 2
            if 0 <= place < ref.shape[0]:
                ref[place] = jump.astype(ref.dtype)

    slopes(patch, w0, 1, deep - 2, to_middle)
    slopes(second, w1, 2, deep - 4, to_jump)


def turn_kernel(host, rows, count, kept, given, last, step, height, *rest):
    outs = 0 if last else 3
    begin = len(rest) - (2 * count + given + outs + kept + 3)
    start, rest = rest[:begin], rest[begin:]
    weights, jumps = rest[:count], rest[count : 2 * count]
    rest = rest[2 * count + given :]
    if not last:
        out, out_top, out_bottom = rest[:3]
        rest = rest[3:]
    saved, (state, *patches) = rest[:kept], rest[kept:]

    @pl.when(lax.axis_index("depth") == host)
    def _():
        halo = (state.shape[0] - rows) // 2
        origin = strip_row(rows) - halo
        if len(start) == 1:
            state[...] = start[0][...]
        else:
            main, top, bottom = start
            state[:halo] = top[...].astype(F32)
            state[halo : halo + rows] = main[...]
            state[halo + rows :] = bottom[...].astype(F32)
        if kept:
            saved[0][...] = state[halo - KEPT : halo + rows + KEPT]
        fill(patches[0], state, rows + 2 * halo, origin, height)
        for k in range(count):
            ends = k == count - 1
            far = 0 if ends and not last else halo - k - 1
            cut = halo - (jumps[k].shape[0] - rows) // 2

            def advance(row, slope):
                new = state[row] + (2.0 * step) * slope + jumps[k][row - cut].astype(F32)
                if k < kept - 1 and halo - KEPT <= row < halo + rows + KEPT:
                    saved[k + 1][row - halo + KEPT] = new
                if not ends:
                    state[row] = new
                    fill_row(patches[(k + 1) % 2], row, new, (origin + row >= 0) & (origin + row < height))
                elif not last:
                    place, edge = row - halo, out_top.shape[0]
                    out[place] = new
                    if place < edge:
                        out_top[place] = new.astype(BF16)
                    if place >= rows - edge:
                        out_bottom[place - rows + edge] = new.astype(BF16)

            slopes(patches[k % 2], weights[k], halo - far, rows + 2 * far, advance)


def pack_kernel(own, core, after, prev, packed, state):
    depth = lax.axis_index("depth")
    final = 4 * ((lax.axis_size("depth") - 1) // 4) + 2
    role = jnp.where(depth < final, depth % 4, depth - final)
    for k, source in enumerate((own, core, after, prev)):

        @pl.when(role == k)
        def _():
            state[...] = source[...]

    ncols = packed.shape[0]
    deep, width, channels = state.shape
    wide = width // ncols
    rows = deep - 2 * KEPT
    first = lax.axis_index("cols") == 0
    group = lax.broadcasted_iota(jnp.int32, (8, channels), 0)
    span = wide + 8
    for k in range(ncols):
        for row in range(rows + KEPT):
            if row < rows:
                line = lambda a, b: state[KEPT + row, a:b]
            else:
                line = lambda a, b: jnp.where(first, state[row - rows, a:b], state[KEPT + row, a:b])
            mine = line(k * wide, (k + 1) * wide)
            right = line((k + 1) * wide, (k + 1) * wide + 8) if k < ncols - 1 else jnp.zeros((8, channels), F32)
            left = line(k * wide - 8, k * wide) if k > 0 else jnp.zeros((8, channels), F32)
            high = mine.astype(BF16)
            packed[k, row * span : row * span + wide] = high
            packed[k, row * span + wide : (row + 1) * span] = jnp.where(group < 4, right, left).astype(BF16)
            if row < rows:
                start = (rows + KEPT) * span + row * wide
                packed[k, start : start + wide] = (mine - high.astype(F32)).astype(BF16)


def tail_kernel(step, height, width, packed, w0, w1, fine, coarse, state, patch, second):
    ncols = packed.shape[0]
    tile_rows, wide = coarse.shape[:2]
    rows = tile_rows // ncols
    span = wide + 8
    for k in range(ncols):
        for row in range(rows):
            start = (rows + KEPT) * span + row * wide
            high = packed[k, row * span : (row + 1) * span].astype(F32)
            whole = high[:wide] + packed[k, start : start + wide].astype(F32)
            place = k * rows + row
            coarse[place] = whole
            state[KEPT + place, :wide] = whole
            state[KEPT + place, wide:] = high[wide:]
    for row in range(KEPT):
        cut = slice((rows + row) * span, (rows + row + 1) * span)
        state[row] = packed[0, cut].astype(F32)
        state[KEPT + tile_rows + row] = packed[ncols - 1, cut].astype(F32)
    top = lax.axis_index("rows") * tile_rows - KEPT
    column = lax.broadcasted_iota(jnp.int32, (span, state.shape[2]), 0)
    place = lax.axis_index("cols") * wide + jnp.where(column < span - 4, column, column - span)
    inside = (place >= 0) & (place < width)
    fill(patch, state, tile_rows + 2 * KEPT, top, height, inside)

    def to_middle(row, slope):
        middle = state[row] + step * slope
        if KEPT <= row < KEPT + tile_rows:
            fine[0, row - KEPT] = middle[:wide]
        fill_row(second, row, middle, (top + row >= 0) & (top + row < height), inside)

    def to_ending(row, slope):
        fine[1, row - KEPT] = fine[0, row - KEPT] + step * slope[:wide]

    slopes(patch, w0, 1, tile_rows + 2, to_middle, 2 * CHUNK)
    slopes(second, w1, 2, tile_rows, to_ending, 2 * CHUNK)


def call(kernel, outs, scratch, inputs, aliases={}, vmem=12 << 20):
    return pl.pallas_call(
        kernel,
        out_shape=[jax.ShapeDtypeStruct(*o) for o in outs],
        in_specs=[pl.BlockSpec(memory_space=pltpu.VMEM)] * len(inputs),
        out_specs=[pl.BlockSpec(memory_space=pltpu.VMEM)] * len(outs),
        scratch_shapes=scratch,
        input_output_aliases=aliases,
        compiler_params=pltpu.CompilerParams(vmem_limit_bytes=vmem),
    )(*inputs)


def on_device(section_states, weights):
    ndepth, nrows, ncols = (lax.axis_size(a) for a in AXES)
    tile = section_states[0]
    tile_rows, tile_cols, channels = tile.shape
    height, width = tile_rows * nrows, tile_cols * ncols
    rows = tile_rows // ncols
    strips = nrows * ncols
    step = 2.0 / (2 * ndepth)
    flat = weights.reshape(2, 3, 3 * channels, channels)
    w0, w1 = flat[0], flat[1]

    hosts = [*range(0, ndepth, 4), ndepth - 2]
    visits = [["own", "core", "next"]] + [["prev", "own", "core", "next"]] * (len(hosts) - 2) + [["own"]]
    visits[-2] = ["prev", "own", "core"]
    halos = [len(v) + 1 for v in visits]
    halos[-1] += 1

    def route(pairs, shift):
        return [
            (a * strips + s, b * strips + (s + shift))
            for a, b in pairs
            for s in range(strips)
            if 0 <= s + shift < strips
        ]

    def fetch(x, slot):
        away = SLOTS[slot]
        return lax.ppermute(x, AXES, route([(h + away, h) for h, v in zip(hosts, visits) if slot in v], 0))

    def ring(x, shift):
        return lax.ppermute(x, ("rows", "cols"), [(s, (s + shift) % strips) for s in range(strips)])

    pieces = lax.all_to_all(tile.reshape(ncols, rows, tile_cols, channels), "cols", 0, 0, tiled=True)
    near = JUMP_HALO["prev"] + 2
    low, high = call(edge_kernel, [((ncols, near, tile_cols, channels), BF16)] * 2, [], (pieces,))
    above, below = ring(high, 1), ring(low, -1)
    far = ("next", "core", "prev")
    all_weights = {"own": w0} | {slot: fetch(w0, slot) for slot in far}
    like = lambda n, t=F32: ((n, width, channels), t)
    vm = lambda n: pltpu.VMEM((n, width, channels), F32)
    patch = lambda n: pltpu.VMEM((n, width, 3 * channels), BF16)
    deep = rows + 2 * near
    kinds = {"prev": BF16, "own": F32, "core": F32, "next": BF16}
    main, top, bottom, *jumps = call(
        functools.partial(head_kernel, step, height),
        [like(rows), like(halos[0], BF16), like(halos[0], BF16)]
        + [like(rows + 2 * JUMP_HALO[slot], kinds[slot]) for slot in SLOTS],
        [vm(deep), vm(deep), patch(deep), patch(deep)],
        (pieces, above, below, w0, w1),
    )
    all_jumps = dict(zip(SLOTS, jumps))
    all_jumps |= {slot: fetch(all_jumps[slot], slot) for slot in far}
    main, top, bottom, all_weights["prev"] = lax.optimization_barrier((main, top, bottom, all_weights["prev"]))

    saved = {}
    start = (main, top, bottom)
    turns = list(zip(hosts, visits, halos))
    turns[:1] = [(hosts[0], visits[0][:-1], halos[0]), (hosts[0], visits[0][-1:], KEPT)]
    for turn, (host, visit, halo) in enumerate(turns):
        last = turn in (0, len(turns) - 1)
        keeps = [] if turn == 1 else [*visit, "next" if turn == 0 else "core"] if last else visit
        given = [slot for slot in keeps if slot in saved]
        outs = [] if last else [like(rows)] + [like(turns[turn + 1][2], BF16)] * 2
        inputs = (
            *start,
            *(all_weights[slot] for slot in visit),
            *(all_jumps[slot] for slot in visit),
            *(saved[slot] for slot in given),
        )
        results = call(
            functools.partial(turn_kernel, host, rows, len(visit), len(keeps), len(given), last, step, height),
            outs + [like(rows + 2 * KEPT)] * len(keeps),
            [vm(rows + 2 * halo), patch(rows + 2 * halo), patch(rows + 2 * halo)],
            inputs,
            {len(inputs) - len(given) + k: len(outs) + keeps.index(slot) for k, slot in enumerate(given)},
        )
        saved |= zip(keeps, results[len(outs) :])
        if turn == 0:
            start = (saved["next"],)
            weight = all_weights["next"]
            (all_weights["next"],) = call(hold_kernel, [(weight.shape, BF16)], [], (weight,))
        elif not last:
            pair = [(host, turns[turn + 1][0])]
            main = lax.ppermute(results[0], AXES, route(pair, 0))
            top = lax.ppermute(results[2], AXES, route(pair, 1))
            bottom = lax.ppermute(results[1], AXES, route(pair, -1))
            start = (main, top, bottom)

    visits[-1] = ["own", "core"]

    def give(slot):
        away = SLOTS[slot]
        return lax.ppermute(saved[slot], AXES, route([(h, h + away) for h, v in zip(hosts, visits) if slot in v], 0))

    span = tile_cols + 8
    pixels = (rows + KEPT) * span + rows * tile_cols
    (packed,) = call(
        pack_kernel,
        [((ncols, pixels, channels), BF16)],
        [vm(rows + 2 * KEPT)],
        (saved["own"], give("core"), give("next"), give("prev")),
    )
    packed = lax.all_to_all(packed, "cols", 0, 0, tiled=True)
    tall = lambda n, t=F32, taps=1: pltpu.VMEM((n, span, taps * channels), t)
    fine, coarse = call(
        functools.partial(tail_kernel, step, height, width),
        [((2, *tile.shape), F32), (tile.shape, F32)],
        [tall(tile_rows + 4), tall(tile_rows + 4, BF16, 3), tall(tile_rows + 4, BF16, 3)],
        (packed, w0, w1),
    )
    return fine, coarse[None]


def solution(mesh):
    in_specs = (P("depth", "rows", "cols", None), P("depth", None, None, None, None))
    out_specs = (P("depth", "rows", "cols", None), P("depth", "rows", "cols", None))
    return jax.shard_map(
        on_device, mesh=mesh, in_specs=in_specs, out_specs=out_specs, check_vma=False
    )
```

```python
import functools

import jax
import jax.numpy as jnp
from jax import lax
from jax.experimental import pallas as pl
from jax.experimental.pallas import tpu as pltpu
from jax.sharding import PartitionSpec as P

AXES = ("depth", "rows", "cols")
BF16 = jnp.bfloat16
F32 = jnp.float32
KEPT = 2
SLOTS = {"prev": -1, "own": 0, "core": 1, "next": 2}
JUMP_HALO = {"prev": 4, "own": 3, "core": 2, "next": 0}


CHUNK = 2


def fill_row(patch, row, x, valid, inside=None):
    width, channels = x.shape
    act = x / (1.0 + jnp.exp(-x))
    act = jnp.where(valid, act, 0.0)
    if inside is not None:
        act = jnp.where(inside, act, 0.0)
    left = pltpu.roll(act, 1, 0)
    right = pltpu.roll(act, width - 1, 0)
    if inside is None:
        column = lax.broadcasted_iota(jnp.int32, (width, channels), 0)
        left = jnp.where(column == 0, 0.0, left)
        right = jnp.where(column == width - 1, 0.0, right)
    for tap, moved in enumerate((left, act, right)):
        patch[row, :, tap * channels : (tap + 1) * channels] = moved.astype(BF16)


def fill(patch, state, rows, first, height, inside=None):
    def body(row, carry):
        fill_row(patch, row, state[row], (first + row >= 0) & (first + row < height), inside)
        return carry

    lax.fori_loop(0, rows, body, 0, unroll=2)


def slopes(patch, weight, first, rows, emit, chunk=CHUNK):
    width, deep = patch.shape[1:]
    for start in range(first, first + rows, chunk):
        count = min(chunk, first + rows - start)
        total = None
        for tap in range(3):
            part = jnp.dot(
                patch[start + tap - 1 : start + tap - 1 + count].reshape(count * width, deep),
                weight[tap],
                preferred_element_type=F32,
            )
            total = part if total is None else total + part
        total = total.reshape(count, width, -1)
        for k in range(count):
            emit(start + k, total[k])


def strip_row(rows):
    return (lax.axis_index("rows") * lax.axis_size("cols") + lax.axis_index("cols")) * rows


def hold_kernel(given, held):
    held[...] = given[...]


def edge_kernel(pieces, low, high):
    rows, count = pieces.shape[1], low.shape[1]
    low[...] = pieces[:, :count].astype(BF16)
    high[...] = pieces[:, rows - count :].astype(BF16)


def head_kernel(step, height, pieces, above, below, w0, layers, main, top, bottom, *rest):
    jumps, (state, first, patch, second, w1, sem) = rest[:-6], rest[-6:]
    load = pltpu.make_async_copy(layers.at[1], w1, sem.at[0])
    load.start()
    ncols, rows, wide = pieces.shape[:3]
    halo = above.shape[1]
    deep = rows + 2 * halo
    origin = strip_row(rows) - halo
    for k in range(ncols):
        cut = slice(k * wide, (k + 1) * wide)
        state[:halo, cut] = above[k].astype(F32)
        state[halo : halo + rows, cut] = pieces[k]
        state[halo + rows :, cut] = below[k].astype(F32)
    main[...] = state[halo : halo + rows]
    top[...] = state[halo - top.shape[0] : halo].astype(BF16)
    bottom[...] = state[halo + rows : halo + rows + bottom.shape[0]].astype(BF16)
    fill(patch, state, deep, origin, height)

    def to_middle(row, slope):
        first[row] = slope
        valid = (origin + row >= 0) & (origin + row < height)
        fill_row(second, row, state[row] + step * slope, valid)

    def to_jump(row, slope):
        jump = step * (slope - first[row])
        for ref in jumps:
            place = row - (deep - ref.shape[0]) // 2
            if 0 <= place < ref.shape[0]:
                ref[place] = jump.astype(ref.dtype)

    slopes(patch, w0, 1, deep - 2, to_middle)
    load.wait()
    slopes(second, w1, 2, deep - 4, to_jump)


def turn_kernel(host, rows, count, kept, given, last, step, height, *rest):
    outs = 0 if last else 4
    begin = len(rest) - (2 * count + given + outs + kept + 3)
    start, rest = rest[:begin], rest[begin:]
    weights, jumps = rest[:count], rest[count : 2 * count]
    rest = rest[2 * count + given :]
    if not last:
        out, out_top, out_bottom, left = rest[:4]
        rest = rest[4:]
    saved, (state, *patches) = rest[:kept], rest[kept:]

    @pl.when(lax.axis_index("depth") == host)
    def _():
        halo = (state.shape[0] - rows) // 2
        origin = strip_row(rows) - halo
        if len(start) == 1:
            state[...] = start[0][...]
        else:
            main, top, bottom = start
            state[:halo] = top[...].astype(F32)
            state[halo : halo + rows] = main[...].astype(F32)
            state[halo + rows :] = bottom[...].astype(F32)
        if kept:
            saved[0][...] = state[halo - KEPT : halo + rows + KEPT]
        fill(patches[0], state, rows + 2 * halo, origin, height)
        for k in range(count):
            ends = k == count - 1
            far = 0 if ends and not last else halo - k - 1
            cut = halo - (jumps[k].shape[0] - rows) // 2

            def advance(row, slope):
                new = state[row] + (2.0 * step) * slope + jumps[k][row - cut].astype(F32)
                if k < kept - 1 and halo - KEPT <= row < halo + rows + KEPT:
                    saved[k + 1][row - halo + KEPT] = new
                if not ends:
                    state[row] = new
                    fill_row(patches[(k + 1) % 2], row, new, (origin + row >= 0) & (origin + row < height))
                elif not last:
                    place, edge = row - halo, out_top.shape[0]
                    high = new.astype(BF16)
                    out[place] = high
                    left[place] = (new - high.astype(F32)).astype(left.dtype)
                    if place < edge:
                        out_top[place] = high
                    if place >= rows - edge:
                        out_bottom[place - rows + edge] = high

            slopes(patches[k % 2], weights[k], halo - far, rows + 2 * far, advance)


def settle_kernel(host, sends, low, *rest):
    if sends:
        left, rest = rest[0], rest[1:]
    kept = len(rest) // 2 if not sends else (len(rest) - 1) // 2
    given, outs = rest[:kept], rest[kept:]

    @pl.when(lax.axis_index("depth") == host)
    def _():
        rows = low.shape[0]
        part = low[...].astype(F32)
        if sends:
            outs[0][...] = (left[...] + part).astype(BF16)
        for old, new in zip(given, outs[1:] if sends else outs):
            new[KEPT : KEPT + rows] = old[KEPT : KEPT + rows] + part


def pack_kernel(own, core, after, prev, packed, state):
    depth = lax.axis_index("depth")
    final = 4 * ((lax.axis_size("depth") - 1) // 4) + 2
    role = jnp.where(depth < final, depth % 4, depth - final)
    for k, source in enumerate((own, core, after, prev)):

        @pl.when(role == k)
        def _():
            state[...] = source[...]

    ncols = packed.shape[0]
    deep, width, channels = state.shape
    wide = width // ncols
    rows = deep - 2 * KEPT
    first = lax.axis_index("cols") == 0
    group = lax.broadcasted_iota(jnp.int32, (8, channels), 0)
    span = wide + 8
    for k in range(ncols):
        for row in range(rows + KEPT):
            if row < rows:
                line = lambda a, b: state[KEPT + row, a:b]
            else:
                line = lambda a, b: jnp.where(first, state[row - rows, a:b], state[KEPT + row, a:b])
            mine = line(k * wide, (k + 1) * wide)
            right = line((k + 1) * wide, (k + 1) * wide + 8) if k < ncols - 1 else jnp.zeros((8, channels), F32)
            left = line(k * wide - 8, k * wide) if k > 0 else jnp.zeros((8, channels), F32)
            high = mine.astype(BF16)
            packed[k, row * span : row * span + wide] = high
            packed[k, row * span + wide : (row + 1) * span] = jnp.where(group < 4, right, left).astype(BF16)
            if row < rows:
                start = (rows + KEPT) * span + row * wide
                packed[k, start : start + wide] = (mine - high.astype(F32)).astype(BF16)


def tail_kernel(step, height, width, packed, layers, fine, coarse, state, patch, second, held, sems):
    loads = [pltpu.make_async_copy(layers.at[k], held.at[k], sems.at[k]) for k in range(2)]
    for load in loads:
        load.start()
    ncols = packed.shape[0]
    tile_rows, wide = coarse.shape[:2]
    rows = tile_rows // ncols
    span = wide + 8
    for k in range(ncols):
        for row in range(rows):
            start = (rows + KEPT) * span + row * wide
            high = packed[k, row * span : (row + 1) * span].astype(F32)
            whole = high[:wide] + packed[k, start : start + wide].astype(F32)
            place = k * rows + row
            coarse[place] = whole
            state[KEPT + place, :wide] = whole
            state[KEPT + place, wide:] = high[wide:]
    for row in range(KEPT):
        cut = slice((rows + row) * span, (rows + row + 1) * span)
        state[row] = packed[0, cut].astype(F32)
        state[KEPT + tile_rows + row] = packed[ncols - 1, cut].astype(F32)
    top = lax.axis_index("rows") * tile_rows - KEPT
    column = lax.broadcasted_iota(jnp.int32, (span, state.shape[2]), 0)
    place = lax.axis_index("cols") * wide + jnp.where(column < span - 4, column, column - span)
    inside = (place >= 0) & (place < width)
    fill(patch, state, tile_rows + 2 * KEPT, top, height, inside)

    def to_middle(row, slope):
        middle = state[row] + step * slope
        if KEPT <= row < KEPT + tile_rows:
            fine[0, row - KEPT] = middle[:wide]
        fill_row(second, row, middle, (top + row >= 0) & (top + row < height), inside)

    def to_ending(row, slope):
        fine[1, row - KEPT] = fine[0, row - KEPT] + step * slope[:wide]

    loads[0].wait()
    slopes(patch, held.at[0], 1, tile_rows + 2, to_middle, 2 * CHUNK)
    loads[1].wait()
    slopes(second, held.at[1], 2, tile_rows, to_ending, 2 * CHUNK)


def call(kernel, outs, scratch, inputs, aliases={}, far=None, vmem=12 << 20, work=0):
    return pl.pallas_call(
        kernel,
        out_shape=[jax.ShapeDtypeStruct(*o) for o in outs],
        in_specs=[pl.BlockSpec(memory_space=pl.ANY if k == far else pltpu.VMEM) for k in range(len(inputs))],
        out_specs=[pl.BlockSpec(memory_space=pltpu.VMEM)] * len(outs),
        scratch_shapes=scratch,
        input_output_aliases=aliases,
        compiler_params=pltpu.CompilerParams(vmem_limit_bytes=vmem),
        cost_estimate=pl.CostEstimate(flops=work, bytes_accessed=0, transcendentals=0) if work else None,
    )(*inputs)


def on_device(section_states, weights):
    ndepth, nrows, ncols = (lax.axis_size(a) for a in AXES)
    tile = section_states[0]
    tile_rows, tile_cols, channels = tile.shape
    height, width = tile_rows * nrows, tile_cols * ncols
    rows = tile_rows // ncols
    strips = nrows * ncols
    step = 2.0 / (2 * ndepth)
    flat = weights.reshape(2, 3, 3 * channels, channels)
    w0 = flat[0]
    held = pltpu.VMEM(w0.shape, BF16)

    hosts = [*range(0, ndepth, 4), ndepth - 2]
    visits = [["own", "core", "next"]] + [["prev", "own", "core", "next"]] * (len(hosts) - 2) + [["own"]]
    visits[-2] = ["prev", "own", "core"]
    halos = [len(v) + 1 for v in visits]
    halos[-1] += 1

    def route(pairs, shift):
        return [
            (a * strips + s, b * strips + (s + shift))
            for a, b in pairs
            for s in range(strips)
            if 0 <= s + shift < strips
        ]

    def fetch(x, slot, only=hosts):
        away = SLOTS[slot]
        pairs = [(h + away, h) for h, v in zip(hosts, visits) if slot in v and h in only]
        return lax.ppermute(x, AXES, route(pairs, 0))

    def ring(x, shift):
        return lax.ppermute(x, ("rows", "cols"), [(s, (s + shift) % strips) for s in range(strips)])

    pieces = lax.all_to_all(tile.reshape(ncols, rows, tile_cols, channels), "cols", 0, 0, tiled=True)
    near = JUMP_HALO["prev"] + 2
    low, high = call(edge_kernel, [((ncols, near, tile_cols, channels), BF16)] * 2, [], (pieces,))
    above, below = ring(high, 1), ring(low, -1)
    far = ("next", "core", "prev")
    all_weights = {"own": w0} | {slot: fetch(w0, slot) for slot in far}
    like = lambda n, t=F32: ((n, width, channels), t)
    vm = lambda n: pltpu.VMEM((n, width, channels), F32)
    patch = lambda n: pltpu.VMEM((n, width, 3 * channels), BF16)
    deep = rows + 2 * near
    kinds = {"prev": BF16, "own": F32, "core": F32, "next": BF16}
    main, top, bottom, *jumps = call(
        functools.partial(head_kernel, step, height),
        [like(rows), like(halos[0], BF16), like(halos[0], BF16)]
        + [like(rows + 2 * JUMP_HALO[slot], kinds[slot]) for slot in SLOTS],
        [vm(deep), vm(deep), patch(deep), patch(deep), held, pltpu.SemaphoreType.DMA((1,))],
        (pieces, above, below, w0, flat),
        far=4,
    )
    all_jumps = dict(zip(SLOTS, jumps))
    first_jump = fetch(all_jumps["next"], "next", hosts[:1])
    all_jumps |= {slot: fetch(all_jumps[slot], slot, hosts[1:] if slot == "next" else hosts) for slot in far}
    main, top, bottom, all_weights["prev"] = lax.optimization_barrier((main, top, bottom, all_weights["prev"]))

    saved = {}
    start = (main, top, bottom)
    turns = list(zip(hosts, visits, halos))
    turns[:1] = [(hosts[0], visits[0][:-1], halos[0]), (hosts[0], visits[0][-1:], KEPT)]
    for turn, (host, visit, halo) in enumerate(turns):
        last = turn in (0, len(turns) - 1)
        keeps = [] if turn == 1 else [*visit, "next" if turn == 0 else "core"] if last else visit
        given = [slot for slot in keeps if slot in saved]
        left = like(rows, BF16 if turn == 1 else F32)
        outs = [] if last else [like(rows, BF16)] + [like(turns[turn + 1][2], BF16)] * 2 + [left]
        inputs = (
            *start,
            *(all_weights[slot] for slot in visit),
            *(first_jump if turn == 1 else all_jumps[slot] for slot in visit),
            *(saved[slot] for slot in given),
        )
        results = call(
            functools.partial(turn_kernel, host, rows, len(visit), len(keeps), len(given), last, step, height),
            outs + [like(rows + 2 * KEPT)] * len(keeps),
            [vm(rows + 2 * halo), patch(rows + 2 * halo), patch(rows + 2 * halo)],
            inputs,
            {len(inputs) - len(given) + k: len(outs) + keeps.index(slot) for k, slot in enumerate(given)},
            work=20_000_000_000 if turn > 1 else 0,
        )
        saved |= zip(keeps, results[len(outs) :])
        if turn == 0:
            start = (saved["next"],)
            weight = all_weights["next"]
            (all_weights["next"],) = call(hold_kernel, [(weight.shape, BF16)], [], (weight,))
            continue
        if turn > 1:
            inputs = (low, *(() if last else results[3:4]), *(saved[slot] for slot in keeps))
            settled = call(
                functools.partial(settle_kernel, host, not last),
                ([] if last else [like(rows, BF16)]) + [like(rows + 2 * KEPT)] * len(keeps),
                [],
                inputs,
                {len(inputs) - len(keeps) + k: int(not last) + k for k in range(len(keeps))},
                work=20_000_000_000,
            )
            saved |= zip(keeps, settled[int(not last) :])
        if not last:
            pair = [(host, turns[turn + 1][0])]
            main = lax.ppermute(results[0], AXES, route(pair, 0))
            top = lax.ppermute(results[2], AXES, route(pair, 1))
            bottom = lax.ppermute(results[1], AXES, route(pair, -1))
            low = lax.ppermute(results[3] if turn == 1 else settled[0], AXES, route(pair, 0))
            start = (main, top, bottom)

    visits[-1] = ["own", "core"]

    def give(slot):
        away = SLOTS[slot]
        return lax.ppermute(saved[slot], AXES, route([(h, h + away) for h, v in zip(hosts, visits) if slot in v], 0))

    span = tile_cols + 8
    pixels = (rows + KEPT) * span + rows * tile_cols
    (packed,) = call(
        pack_kernel,
        [((ncols, pixels, channels), BF16)],
        [vm(rows + 2 * KEPT)],
        (saved["own"], give("core"), give("next"), give("prev")),
    )
    packed = lax.all_to_all(packed, "cols", 0, 0, tiled=True)
    tall = lambda n, t=F32, taps=1: pltpu.VMEM((n, span, taps * channels), t)
    fine, coarse = call(
        functools.partial(tail_kernel, step, height, width),
        [((2, *tile.shape), F32), (tile.shape, F32)],
        [tall(tile_rows + 4), tall(tile_rows + 4, BF16, 3), tall(tile_rows + 4, BF16, 3)]
        + [pltpu.VMEM(flat.shape, BF16), pltpu.SemaphoreType.DMA((2,))],
        (packed, flat),
        far=1,
    )
    return fine, coarse[None]


def solution(mesh):
    in_specs = (P("depth", "rows", "cols", None), P("depth", None, None, None, None))
    out_specs = (P("depth", "rows", "cols", None), P("depth", "rows", "cols", None))
    return jax.shard_map(
        on_device, mesh=mesh, in_specs=in_specs, out_specs=out_specs, check_vma=False
    )
```

```python
import functools

import jax
import jax.numpy as jnp
from jax import lax
from jax.experimental import pallas as pl
from jax.experimental.pallas import tpu as pltpu
from jax.sharding import PartitionSpec as P

AXES = ("depth", "rows", "cols")
BF16 = jnp.bfloat16
F32 = jnp.float32
KEPT = 2
SLOTS = {"prev": -1, "own": 0, "core": 1, "next": 2}
JUMP_HALO = {"prev": 4, "own": 3, "core": 2, "next": 0}


CHUNK = 2


def fill_row(patch, row, x, valid, inside=None):
    width, channels = x.shape
    act = x / (1.0 + jnp.exp(-x))
    act = jnp.where(valid, act, 0.0)
    if inside is not None:
        act = jnp.where(inside, act, 0.0)
    left = pltpu.roll(act, 1, 0)
    right = pltpu.roll(act, width - 1, 0)
    if inside is None:
        column = lax.broadcasted_iota(jnp.int32, (width, channels), 0)
        left = jnp.where(column == 0, 0.0, left)
        right = jnp.where(column == width - 1, 0.0, right)
    for tap, moved in enumerate((left, act, right)):
        patch[row, :, tap * channels : (tap + 1) * channels] = moved.astype(BF16)


def fill(patch, state, rows, first, height, inside=None):
    def body(row, carry):
        fill_row(patch, row, state[row], (first + row >= 0) & (first + row < height), inside)
        return carry

    lax.fori_loop(0, rows, body, 0, unroll=2)


def slopes(patch, weight, first, rows, emit, chunk=CHUNK):
    width, deep = patch.shape[1:]
    for start in range(first, first + rows, chunk):
        count = min(chunk, first + rows - start)
        total = None
        for tap in range(3):
            part = jnp.dot(
                patch[start + tap - 1 : start + tap - 1 + count].reshape(count * width, deep),
                weight[tap],
                preferred_element_type=F32,
            )
            total = part if total is None else total + part
        total = total.reshape(count, width, -1)
        for k in range(count):
            emit(start + k, total[k])


def strip_row(rows):
    return (lax.axis_index("rows") * lax.axis_size("cols") + lax.axis_index("cols")) * rows


def edge_kernel(pieces, low, high):
    rows, count = pieces.shape[1], low.shape[1]
    low[...] = pieces[:, :count].astype(BF16)
    high[...] = pieces[:, rows - count :].astype(BF16)


def head_kernel(step, height, pieces, above, below, layers, main, top, bottom, *rest):
    jumps, (state, first, patch, second) = rest[:-4], rest[-4:]
    ncols, rows, wide = pieces.shape[:3]
    halo = above.shape[1]
    deep = rows + 2 * halo
    origin = strip_row(rows) - halo
    for k in range(ncols):
        cut = slice(k * wide, (k + 1) * wide)
        state[:halo, cut] = above[k].astype(F32)
        state[halo : halo + rows, cut] = pieces[k]
        state[halo + rows :, cut] = below[k].astype(F32)
    main[...] = state[halo : halo + rows]
    top[...] = state[halo - top.shape[0] : halo].astype(BF16)
    bottom[...] = state[halo + rows : halo + rows + bottom.shape[0]].astype(BF16)
    fill(patch, state, deep, origin, height)

    def to_middle(row, slope):
        first[row] = slope
        valid = (origin + row >= 0) & (origin + row < height)
        fill_row(second, row, state[row] + step * slope, valid)

    def to_jump(row, slope):
        jump = step * (slope - first[row])
        for ref in jumps:
            place = row - (deep - ref.shape[0]) // 2
            if 0 <= place < ref.shape[0]:
                ref[place] = jump.astype(ref.dtype)

    slopes(patch, layers.at[0], 1, deep - 2, to_middle)
    slopes(second, layers.at[1], 2, deep - 4, to_jump)


def turn_kernel(host, rows, count, kept, given, last, step, height, *rest):
    outs = 0 if last else 4
    begin = len(rest) - (2 * count + given + outs + kept + 3)
    start, rest = rest[:begin], rest[begin:]
    weights, jumps = rest[:count], rest[count : 2 * count]
    weights = [weight.at[0] if len(weight.shape) == 4 else weight for weight in weights]
    rest = rest[2 * count + given :]
    if not last:
        out, out_top, out_bottom, left = rest[:4]
        rest = rest[4:]
    saved, (state, *patches) = rest[:kept], rest[kept:]

    @pl.when(lax.axis_index("depth") == host)
    def _():
        halo = (state.shape[0] - rows) // 2
        origin = strip_row(rows) - halo
        if len(start) == 1:
            state[...] = start[0][...]
        else:
            main, top, bottom = start
            state[:halo] = top[...].astype(F32)
            state[halo : halo + rows] = main[...].astype(F32)
            state[halo + rows :] = bottom[...].astype(F32)
        if kept:
            saved[0][...] = state[halo - KEPT : halo + rows + KEPT]
        fill(patches[0], state, rows + 2 * halo, origin, height)
        for k in range(count):
            ends = k == count - 1
            far = 0 if ends and not last else halo - k - 1
            cut = halo - (jumps[k].shape[0] - rows) // 2

            def advance(row, slope):
                new = state[row] + (2.0 * step) * slope + jumps[k][row - cut].astype(F32)
                if k < kept - 1 and halo - KEPT <= row < halo + rows + KEPT:
                    saved[k + 1][row - halo + KEPT] = new
                if not ends:
                    state[row] = new
                    fill_row(patches[(k + 1) % 2], row, new, (origin + row >= 0) & (origin + row < height))
                elif not last:
                    place, edge = row - halo, out_top.shape[0]
                    high = new.astype(BF16)
                    out[place] = high
                    left[place] = (new - high.astype(F32)).astype(left.dtype)
                    if place < edge:
                        out_top[place] = high
                    if place >= rows - edge:
                        out_bottom[place - rows + edge] = high

            slopes(patches[k % 2], weights[k], halo - far, rows + 2 * far, advance)


def settle_kernel(host, sends, low, *rest):
    if sends:
        left, rest = rest[0], rest[1:]
    kept = len(rest) // 2 if not sends else (len(rest) - 1) // 2
    given, outs = rest[:kept], rest[kept:]

    @pl.when(lax.axis_index("depth") == host)
    def _():
        rows = low.shape[0]
        part = low[...].astype(F32)
        if sends:
            outs[0][...] = (left[...] + part).astype(BF16)
        for old, new in zip(given, outs[1:] if sends else outs):
            new[KEPT : KEPT + rows] = old[KEPT : KEPT + rows] + part


def pack_kernel(own, core, after, prev, packed, state):
    depth = lax.axis_index("depth")
    final = 4 * ((lax.axis_size("depth") - 1) // 4) + 2
    role = jnp.where(depth < final, depth % 4, depth - final)
    for k, source in enumerate((own, core, after, prev)):

        @pl.when(role == k)
        def _():
            state[...] = source[...]

    ncols = packed.shape[0]
    deep, width, channels = state.shape
    wide = width // ncols
    rows = deep - 2 * KEPT
    first = lax.axis_index("cols") == 0
    group = lax.broadcasted_iota(jnp.int32, (8, channels), 0)
    span = wide + 8
    for k in range(ncols):
        for row in range(rows + KEPT):
            if row < rows:
                line = lambda a, b: state[KEPT + row, a:b]
            else:
                line = lambda a, b: jnp.where(first, state[row - rows, a:b], state[KEPT + row, a:b])
            mine = line(k * wide, (k + 1) * wide)
            right = line((k + 1) * wide, (k + 1) * wide + 8) if k < ncols - 1 else jnp.zeros((8, channels), F32)
            left = line(k * wide - 8, k * wide) if k > 0 else jnp.zeros((8, channels), F32)
            high = mine.astype(BF16)
            packed[k, row * span : row * span + wide] = high
            packed[k, row * span + wide : (row + 1) * span] = jnp.where(group < 4, right, left).astype(BF16)
            if row < rows:
                start = (rows + KEPT) * span + row * wide
                packed[k, start : start + wide] = (mine - high.astype(F32)).astype(BF16)


def tail_kernel(step, height, width, packed, layers, fine, coarse, state, patch, second):
    ncols = packed.shape[0]
    tile_rows, wide = coarse.shape[:2]
    rows = tile_rows // ncols
    span = wide + 8
    for k in range(ncols):
        for row in range(rows):
            start = (rows + KEPT) * span + row * wide
            high = packed[k, row * span : (row + 1) * span].astype(F32)
            whole = high[:wide] + packed[k, start : start + wide].astype(F32)
            place = k * rows + row
            coarse[place] = whole
            state[KEPT + place, :wide] = whole
            state[KEPT + place, wide:] = high[wide:]
    for row in range(KEPT):
        cut = slice((rows + row) * span, (rows + row + 1) * span)
        state[row] = packed[0, cut].astype(F32)
        state[KEPT + tile_rows + row] = packed[ncols - 1, cut].astype(F32)
    top = lax.axis_index("rows") * tile_rows - KEPT
    column = lax.broadcasted_iota(jnp.int32, (span, state.shape[2]), 0)
    place = lax.axis_index("cols") * wide + jnp.where(column < span - 4, column, column - span)
    inside = (place >= 0) & (place < width)
    fill(patch, state, tile_rows + 2 * KEPT, top, height, inside)

    def to_middle(row, slope):
        middle = state[row] + step * slope
        if KEPT <= row < KEPT + tile_rows:
            fine[0, row - KEPT] = middle[:wide]
        fill_row(second, row, middle, (top + row >= 0) & (top + row < height), inside)

    def to_ending(row, slope):
        fine[1, row - KEPT] = fine[0, row - KEPT] + step * slope[:wide]

    slopes(patch, layers.at[0], 1, tile_rows + 2, to_middle, 2 * CHUNK)
    slopes(second, layers.at[1], 2, tile_rows, to_ending, 2 * CHUNK)


def call(kernel, outs, scratch, inputs, aliases={}, vmem=12 << 20, work=0):
    return pl.pallas_call(
        kernel,
        out_shape=[jax.ShapeDtypeStruct(*o) for o in outs],
        in_specs=[pl.BlockSpec(memory_space=pltpu.VMEM)] * len(inputs),
        out_specs=[pl.BlockSpec(memory_space=pltpu.VMEM)] * len(outs),
        scratch_shapes=scratch,
        input_output_aliases=aliases,
        compiler_params=pltpu.CompilerParams(vmem_limit_bytes=vmem),
        cost_estimate=pl.CostEstimate(flops=work, bytes_accessed=0, transcendentals=0) if work else None,
    )(*inputs)


def on_device(section_states, weights):
    ndepth, nrows, ncols = (lax.axis_size(a) for a in AXES)
    tile = section_states[0]
    tile_rows, tile_cols, channels = tile.shape
    height, width = tile_rows * nrows, tile_cols * ncols
    rows = tile_rows // ncols
    strips = nrows * ncols
    step = 2.0 / (2 * ndepth)
    flat = weights.reshape(2, 3, 3 * channels, channels)
    w0 = flat[0]

    hosts = [*range(0, ndepth, 4), ndepth - 2]
    visits = [["own", "core", "next"]] + [["prev", "own", "core", "next"]] * (len(hosts) - 2) + [["own"]]
    visits[-2] = ["prev", "own", "core"]
    halos = [len(v) + 1 for v in visits]
    halos[-1] += 1

    def route(pairs, shift):
        return [
            (a * strips + s, b * strips + (s + shift))
            for a, b in pairs
            for s in range(strips)
            if 0 <= s + shift < strips
        ]

    def fetch(x, slot, only=hosts):
        away = SLOTS[slot]
        pairs = [(h + away, h) for h, v in zip(hosts, visits) if slot in v and h in only]
        return lax.ppermute(x, AXES, route(pairs, 0))

    def ring(x, shift):
        return lax.ppermute(x, ("rows", "cols"), [(s, (s + shift) % strips) for s in range(strips)])

    pieces = lax.all_to_all(tile.reshape(ncols, rows, tile_cols, channels), "cols", 0, 0, tiled=True)
    near = JUMP_HALO["prev"] + 2
    low, high = call(edge_kernel, [((ncols, near, tile_cols, channels), BF16)] * 2, [], (pieces,))
    above, below = ring(high, 1), ring(low, -1)
    far = ("next", "core", "prev")
    all_weights = {"own": flat} | {slot: fetch(w0, slot) for slot in far}
    like = lambda n, t=F32: ((n, width, channels), t)
    vm = lambda n: pltpu.VMEM((n, width, channels), F32)
    patch = lambda n: pltpu.VMEM((n, width, 3 * channels), BF16)
    deep = rows + 2 * near
    kinds = {"prev": BF16, "own": F32, "core": F32, "next": BF16}
    main, top, bottom, *jumps = call(
        functools.partial(head_kernel, step, height),
        [like(rows), like(halos[0], BF16), like(halos[0], BF16)]
        + [like(rows + 2 * JUMP_HALO[slot], kinds[slot]) for slot in SLOTS],
        [vm(deep), vm(deep), patch(deep), patch(deep)],
        (pieces, above, below, flat),
        work=10_000_000_000,
    )
    all_jumps = dict(zip(SLOTS, jumps))
    first_jump = fetch(all_jumps["next"], "next", hosts[:1])
    all_jumps |= {slot: fetch(all_jumps[slot], slot, hosts[1:] if slot == "next" else hosts) for slot in far}
    main, top, bottom, all_weights["prev"] = lax.optimization_barrier((main, top, bottom, all_weights["prev"]))

    saved = {}
    start = (main, top, bottom)
    turns = list(zip(hosts, visits, halos))
    turns[:1] = [(hosts[0], visits[0][:-1], halos[0]), (hosts[0], visits[0][-1:], KEPT)]
    for turn, (host, visit, halo) in enumerate(turns):
        last = turn in (0, len(turns) - 1)
        keeps = [] if turn == 1 else [*visit, "next" if turn == 0 else "core"] if last else visit
        given = [slot for slot in keeps if slot in saved]
        left = like(rows, BF16 if turn == 1 else F32)
        outs = [] if last else [like(rows, BF16)] + [like(turns[turn + 1][2], BF16)] * 2 + [left]
        inputs = (
            *start,
            *(all_weights[slot] for slot in visit),
            *(first_jump if turn == 1 else all_jumps[slot] for slot in visit),
            *(saved[slot] for slot in given),
        )
        results = call(
            functools.partial(turn_kernel, host, rows, len(visit), len(keeps), len(given), last, step, height),
            outs + [like(rows + 2 * KEPT)] * len(keeps),
            [vm(rows + 2 * halo), patch(rows + 2 * halo), patch(rows + 2 * halo)],
            inputs,
            {len(inputs) - len(given) + k: len(outs) + keeps.index(slot) for k, slot in enumerate(given)},
            work=20_000_000_000 if turn > 1 else 0,
        )
        saved |= zip(keeps, results[len(outs) :])
        if turn == 0:
            start = (saved["next"],)
            continue
        if turn > 1:
            inputs = (low, *(() if last else results[3:4]), *(saved[slot] for slot in keeps))
            settled = call(
                functools.partial(settle_kernel, host, not last),
                ([] if last else [like(rows, BF16)]) + [like(rows + 2 * KEPT)] * len(keeps),
                [],
                inputs,
                {len(inputs) - len(keeps) + k: int(not last) + k for k in range(len(keeps))},
                work=20_000_000_000,
            )
            saved |= zip(keeps, settled[int(not last) :])
        if not last:
            pair = [(host, turns[turn + 1][0])]
            main = lax.ppermute(results[0], AXES, route(pair, 0))
            top = lax.ppermute(results[2], AXES, route(pair, 1))
            bottom = lax.ppermute(results[1], AXES, route(pair, -1))
            low = lax.ppermute(results[3] if turn == 1 else settled[0], AXES, route(pair, 0))
            start = (main, top, bottom)

    visits[-1] = ["own", "core"]

    def give(slot):
        away = SLOTS[slot]
        return lax.ppermute(saved[slot], AXES, route([(h, h + away) for h, v in zip(hosts, visits) if slot in v], 0))

    span = tile_cols + 8
    pixels = (rows + KEPT) * span + rows * tile_cols
    (packed,) = call(
        pack_kernel,
        [((ncols, pixels, channels), BF16)],
        [vm(rows + 2 * KEPT)],
        (saved["own"], give("core"), give("next"), give("prev")),
    )
    packed = lax.all_to_all(packed, "cols", 0, 0, tiled=True)
    tall = lambda n, t=F32, taps=1: pltpu.VMEM((n, span, taps * channels), t)
    fine, coarse = call(
        functools.partial(tail_kernel, step, height, width),
        [((2, *tile.shape), F32), (tile.shape, F32)],
        [tall(tile_rows + 4), tall(tile_rows + 4, BF16, 3), tall(tile_rows + 4, BF16, 3)],
        (packed, flat),
    )
    return fine, coarse[None]


def solution(mesh):
    in_specs = (P("depth", "rows", "cols", None), P("depth", None, None, None, None))
    out_specs = (P("depth", "rows", "cols", None), P("depth", "rows", "cols", None))
    return jax.shard_map(
        on_device, mesh=mesh, in_specs=in_specs, out_specs=out_specs, check_vma=False
    )
```

```python
import functools

import jax
import jax.numpy as jnp
from jax import lax
from jax.experimental import pallas as pl
from jax.experimental.pallas import tpu as pltpu
from jax.sharding import PartitionSpec as P

AXES = ("depth", "rows", "cols")
BF16 = jnp.bfloat16
F32 = jnp.float32
KEPT = 2
SLOTS = {"prev": -1, "own": 0, "core": 1, "next": 2}
JUMP_HALO = {"prev": 4, "own": 3, "core": 2, "next": 0}


CHUNK = 2


def fill_row(patch, row, x, valid, inside=None):
    width, channels = x.shape
    act = x / (1.0 + jnp.exp(-x))
    act = jnp.where(valid, act, 0.0)
    if inside is not None:
        act = jnp.where(inside, act, 0.0)
    left = pltpu.roll(act, 1, 0)
    right = pltpu.roll(act, width - 1, 0)
    if inside is None:
        column = lax.broadcasted_iota(jnp.int32, (width, channels), 0)
        left = jnp.where(column == 0, 0.0, left)
        right = jnp.where(column == width - 1, 0.0, right)
    for tap, moved in enumerate((left, act, right)):
        patch[row, :, tap * channels : (tap + 1) * channels] = moved.astype(BF16)


def fill(patch, state, rows, first, height, inside=None):
    def body(row, carry):
        fill_row(patch, row, state[row], (first + row >= 0) & (first + row < height), inside)
        return carry

    lax.fori_loop(0, rows, body, 0, unroll=2)


def slopes(patch, weight, first, rows, emit, chunk=CHUNK):
    width, deep = patch.shape[1:]
    for start in range(first, first + rows, chunk):
        count = min(chunk, first + rows - start)
        total = None
        for tap in range(3):
            part = jnp.dot(
                patch[start + tap - 1 : start + tap - 1 + count].reshape(count * width, deep),
                weight[tap],
                preferred_element_type=F32,
            )
            total = part if total is None else total + part
        total = total.reshape(count, width, -1)
        for k in range(count):
            emit(start + k, total[k])


def strip_row(rows):
    return (lax.axis_index("rows") * lax.axis_size("cols") + lax.axis_index("cols")) * rows


def edge_kernel(pieces, low, high):
    rows, count = pieces.shape[1], low.shape[1]
    low[...] = pieces[:, :count].astype(BF16)
    high[...] = pieces[:, rows - count :].astype(BF16)


def head_kernel(step, height, pieces, above, below, layers, main, top, bottom, *rest):
    jumps, (state, first, patch, second) = rest[:-4], rest[-4:]
    ncols, rows, wide = pieces.shape[:3]
    halo = above.shape[1]
    deep = rows + 2 * halo
    origin = strip_row(rows) - halo
    for k in range(ncols):
        cut = slice(k * wide, (k + 1) * wide)
        state[:halo, cut] = above[k].astype(F32)
        state[halo : halo + rows, cut] = pieces[k]
        state[halo + rows :, cut] = below[k].astype(F32)
    main[...] = state[halo : halo + rows]
    top[...] = state[halo - top.shape[0] : halo].astype(BF16)
    bottom[...] = state[halo + rows : halo + rows + bottom.shape[0]].astype(BF16)
    fill(patch, state, deep, origin, height)

    def to_middle(row, slope):
        first[row] = slope
        valid = (origin + row >= 0) & (origin + row < height)
        fill_row(second, row, state[row] + step * slope, valid)

    def to_jump(row, slope):
        jump = step * (slope - first[row])
        for ref in jumps:
            place = row - (deep - ref.shape[0]) // 2
            if 0 <= place < ref.shape[0]:
                ref[place] = jump.astype(ref.dtype)

    slopes(patch, layers.at[0], 1, deep - 2, to_middle)
    slopes(second, layers.at[1], 2, deep - 4, to_jump)


def turn_kernel(host, rows, count, kept, given, last, step, height, *rest):
    outs = 0 if last else 4
    begin = len(rest) - (2 * count + given + outs + kept + 3)
    start, rest = rest[:begin], rest[begin:]
    weights, jumps = rest[:count], rest[count : 2 * count]
    weights = [weight.at[0] if len(weight.shape) == 4 else weight for weight in weights]
    rest = rest[2 * count + given :]
    if not last:
        out, out_top, out_bottom, left = rest[:4]
        rest = rest[4:]
    saved, (state, *patches) = rest[:kept], rest[kept:]

    @pl.when(lax.axis_index("depth") == host)
    def _():
        halo = (state.shape[0] - rows) // 2
        origin = strip_row(rows) - halo
        if len(start) == 1:
            state[...] = start[0][...]
        else:
            main, top, bottom = start
            state[:halo] = top[...].astype(F32)
            state[halo : halo + rows] = main[...].astype(F32)
            state[halo + rows :] = bottom[...].astype(F32)
        if kept:
            saved[0][...] = state[halo - KEPT : halo + rows + KEPT]
        fill(patches[0], state, rows + 2 * halo, origin, height)
        for k in range(count):
            ends = k == count - 1
            far = 0 if ends and not last else halo - k - 1
            cut = halo - (jumps[k].shape[0] - rows) // 2

            def advance(row, slope):
                new = state[row] + (2.0 * step) * slope + jumps[k][row - cut].astype(F32)
                if k < kept - 1 and halo - KEPT <= row < halo + rows + KEPT:
                    saved[k + 1][row - halo + KEPT] = new
                if not ends:
                    state[row] = new
                    fill_row(patches[(k + 1) % 2], row, new, (origin + row >= 0) & (origin + row < height))
                elif not last:
                    place, edge = row - halo, out_top.shape[0]
                    high = new.astype(BF16)
                    out[place] = high
                    left[place] = (new - high.astype(F32)).astype(left.dtype)
                    if place < edge:
                        out_top[place] = high
                    if place >= rows - edge:
                        out_bottom[place - rows + edge] = high

            slopes(patches[k % 2], weights[k], halo - far, rows + 2 * far, advance)


def settle_kernel(host, sends, low, *rest):
    if sends:
        left, rest = rest[0], rest[1:]
    kept = len(rest) // 2 if not sends else (len(rest) - 1) // 2
    given, outs = rest[:kept], rest[kept:]

    @pl.when(lax.axis_index("depth") == host)
    def _():
        rows = low.shape[0]
        part = low[...].astype(F32)
        if sends:
            outs[0][...] = (left[...] + part).astype(BF16)
        for old, new in zip(given, outs[1:] if sends else outs):
            new[KEPT : KEPT + rows] = old[KEPT : KEPT + rows] + part


def pack_kernel(own, core, after, prev, packed, state):
    depth = lax.axis_index("depth")
    final = 4 * ((lax.axis_size("depth") - 1) // 4) + 2
    role = jnp.where(depth < final, depth % 4, depth - final)
    for k, source in enumerate((own, core, after, prev)):

        @pl.when(role == k)
        def _():
            state[...] = source[...]

    ncols = packed.shape[0]
    deep, width, channels = state.shape
    wide = width // ncols
    rows = deep - 2 * KEPT
    first = lax.axis_index("cols") == 0
    group = lax.broadcasted_iota(jnp.int32, (8, channels), 0)
    span = wide + 8
    for k in range(ncols):
        for row in range(rows + KEPT):
            if row < rows:
                line = lambda a, b: state[KEPT + row, a:b]
            else:
                line = lambda a, b: jnp.where(first, state[row - rows, a:b], state[KEPT + row, a:b])
            mine = line(k * wide, (k + 1) * wide)
            right = line((k + 1) * wide, (k + 1) * wide + 8) if k < ncols - 1 else jnp.zeros((8, channels), F32)
            left = line(k * wide - 8, k * wide) if k > 0 else jnp.zeros((8, channels), F32)
            high = mine.astype(BF16)
            packed[k, row * span : row * span + wide] = high
            packed[k, row * span + wide : (row + 1) * span] = jnp.where(group < 4, right, left).astype(BF16)
            if row < rows:
                start = (rows + KEPT) * span + row * wide
                packed[k, start : start + wide] = (mine - high.astype(F32)).astype(BF16)


def tail_kernel(step, height, width, packed, layers, fine, coarse, state, patch, second):
    ncols = packed.shape[0]
    tile_rows, wide = coarse.shape[:2]
    rows = tile_rows // ncols
    span = wide + 8
    for k in range(ncols):
        for row in range(rows):
            start = (rows + KEPT) * span + row * wide
            high = packed[k, row * span : (row + 1) * span].astype(F32)
            whole = high[:wide] + packed[k, start : start + wide].astype(F32)
            place = k * rows + row
            coarse[place] = whole
            state[KEPT + place, :wide] = whole
            state[KEPT + place, wide:] = high[wide:]
    for row in range(KEPT):
        cut = slice((rows + row) * span, (rows + row + 1) * span)
        state[row] = packed[0, cut].astype(F32)
        state[KEPT + tile_rows + row] = packed[ncols - 1, cut].astype(F32)
    top = lax.axis_index("rows") * tile_rows - KEPT
    column = lax.broadcasted_iota(jnp.int32, (span, state.shape[2]), 0)
    place = lax.axis_index("cols") * wide + jnp.where(column < span - 4, column, column - span)
    inside = (place >= 0) & (place < width)
    fill(patch, state, tile_rows + 2 * KEPT, top, height, inside)

    def to_middle(row, slope):
        middle = state[row] + step * slope
        if KEPT <= row < KEPT + tile_rows:
            fine[0, row - KEPT] = middle[:wide]
        fill_row(second, row, middle, (top + row >= 0) & (top + row < height), inside)

    def to_ending(row, slope):
        fine[1, row - KEPT] = fine[0, row - KEPT] + step * slope[:wide]

    slopes(patch, layers.at[0], 1, tile_rows + 2, to_middle, 2 * CHUNK)
    slopes(second, layers.at[1], 2, tile_rows, to_ending, 2 * CHUNK)


def call(kernel, outs, scratch, inputs, aliases={}, vmem=12 << 20, work=0):
    return pl.pallas_call(
        kernel,
        out_shape=[jax.ShapeDtypeStruct(*o) for o in outs],
        in_specs=[pl.BlockSpec(memory_space=pltpu.VMEM)] * len(inputs),
        out_specs=[pl.BlockSpec(memory_space=pltpu.VMEM)] * len(outs),
        scratch_shapes=scratch,
        input_output_aliases=aliases,
        compiler_params=pltpu.CompilerParams(vmem_limit_bytes=vmem),
        cost_estimate=pl.CostEstimate(flops=work, bytes_accessed=0, transcendentals=0) if work else None,
    )(*inputs)


def on_device(section_states, weights):
    ndepth, nrows, ncols = (lax.axis_size(a) for a in AXES)
    tile = section_states[0]
    tile_rows, tile_cols, channels = tile.shape
    height, width = tile_rows * nrows, tile_cols * ncols
    rows = tile_rows // ncols
    strips = nrows * ncols
    step = 2.0 / (2 * ndepth)
    flat = weights.reshape(2, 3, 3 * channels, channels)
    w0 = flat[0]

    hosts = [*range(0, ndepth, 4), ndepth - 2]
    visits = [["own", "core", "next"]] + [["prev", "own", "core", "next"]] * (len(hosts) - 2) + [["own"]]
    visits[-2] = ["prev", "own", "core"]
    halos = [len(v) + 1 for v in visits]
    halos[-1] += 1

    def route(pairs, shift):
        return [
            (a * strips + s, b * strips + (s + shift))
            for a, b in pairs
            for s in range(strips)
            if 0 <= s + shift < strips
        ]

    def fetch(x, slot, only=hosts):
        away = SLOTS[slot]
        pairs = [(h + away, h) for h, v in zip(hosts, visits) if slot in v and h in only]
        return lax.ppermute(x, AXES, route(pairs, 0))

    def ring(x, shift):
        return lax.ppermute(x, ("rows", "cols"), [(s, (s + shift) % strips) for s in range(strips)])

    pieces = lax.all_to_all(tile.reshape(ncols, rows, tile_cols, channels), "cols", 0, 0, tiled=True)
    near = JUMP_HALO["prev"] + 2
    low, high = call(edge_kernel, [((ncols, near, tile_cols, channels), BF16)] * 2, [], (pieces,))
    above, below = ring(high, 1), ring(low, -1)
    far = ("next", "core", "prev")
    all_weights = {"own": flat} | {slot: fetch(w0, slot) for slot in far}
    like = lambda n, t=F32: ((n, width, channels), t)
    vm = lambda n: pltpu.VMEM((n, width, channels), F32)
    patch = lambda n: pltpu.VMEM((n, width, 3 * channels), BF16)
    deep = rows + 2 * near
    kinds = {"prev": BF16, "own": F32, "core": F32, "next": BF16}
    main, top, bottom, *jumps = call(
        functools.partial(head_kernel, step, height),
        [like(rows), like(halos[0], BF16), like(halos[0], BF16)]
        + [like(rows + 2 * JUMP_HALO[slot], kinds[slot]) for slot in SLOTS],
        [vm(deep), vm(deep), patch(deep), patch(deep)],
        (pieces, above, below, flat),
        work=15_000_000_000,
    )
    *jumps, all_weights["core"] = lax.optimization_barrier((*jumps, all_weights["core"]))
    all_jumps = dict(zip(SLOTS, jumps))
    first_jump = fetch(all_jumps["next"], "next", hosts[:1])
    all_jumps |= {slot: fetch(all_jumps[slot], slot, hosts[1:] if slot == "next" else hosts) for slot in far}

    saved = {}
    start = (main, top, bottom)
    turns = list(zip(hosts, visits, halos))
    turns[:1] = [(hosts[0], visits[0][:-1], halos[0]), (hosts[0], visits[0][-1:], KEPT)]
    for turn, (host, visit, halo) in enumerate(turns):
        last = turn in (0, len(turns) - 1)
        keeps = [] if turn == 1 else [*visit, "next" if turn == 0 else "core"] if last else visit
        given = [slot for slot in keeps if slot in saved]
        left = like(rows, BF16 if turn == 1 else F32)
        outs = [] if last else [like(rows, BF16)] + [like(turns[turn + 1][2], BF16)] * 2 + [left]
        inputs = (
            *start,
            *(all_weights[slot] for slot in visit),
            *(first_jump if turn == 1 else all_jumps[slot] for slot in visit),
            *(saved[slot] for slot in given),
        )
        results = call(
            functools.partial(turn_kernel, host, rows, len(visit), len(keeps), len(given), last, step, height),
            outs + [like(rows + 2 * KEPT)] * len(keeps),
            [vm(rows + 2 * halo), patch(rows + 2 * halo), patch(rows + 2 * halo)],
            inputs,
            {len(inputs) - len(given) + k: len(outs) + keeps.index(slot) for k, slot in enumerate(given)},
            work=20_000_000_000 if turn > 1 else 0,
        )
        saved |= zip(keeps, results[len(outs) :])
        if turn == 0:
            start = (saved["next"],)
            continue
        if turn > 1:
            inputs = (low, *(() if last else results[3:4]), *(saved[slot] for slot in keeps))
            settled = call(
                functools.partial(settle_kernel, host, not last),
                ([] if last else [like(rows, BF16)]) + [like(rows + 2 * KEPT)] * len(keeps),
                [],
                inputs,
                {len(inputs) - len(keeps) + k: int(not last) + k for k in range(len(keeps))},
                work=20_000_000_000,
            )
            saved |= zip(keeps, settled[int(not last) :])
        if not last:
            pair = [(host, turns[turn + 1][0])]
            main = lax.ppermute(results[0], AXES, route(pair, 0))
            top = lax.ppermute(results[2], AXES, route(pair, 1))
            bottom = lax.ppermute(results[1], AXES, route(pair, -1))
            low = lax.ppermute(results[3] if turn == 1 else settled[0], AXES, route(pair, 0))
            start = (main, top, bottom)

    visits[-1] = ["own", "core"]

    def give(slot):
        away = SLOTS[slot]
        return lax.ppermute(saved[slot], AXES, route([(h, h + away) for h, v in zip(hosts, visits) if slot in v], 0))

    span = tile_cols + 8
    pixels = (rows + KEPT) * span + rows * tile_cols
    (packed,) = call(
        pack_kernel,
        [((ncols, pixels, channels), BF16)],
        [vm(rows + 2 * KEPT)],
        (saved["own"], give("core"), give("next"), give("prev")),
    )
    packed = lax.all_to_all(packed, "cols", 0, 0, tiled=True)
    tall = lambda n, t=F32, taps=1: pltpu.VMEM((n, span, taps * channels), t)
    fine, coarse = call(
        functools.partial(tail_kernel, step, height, width),
        [((2, *tile.shape), F32), (tile.shape, F32)],
        [tall(tile_rows + 4), tall(tile_rows + 4, BF16, 3), tall(tile_rows + 4, BF16, 3)],
        (packed, flat),
    )
    return fine, coarse[None]


def solution(mesh):
    in_specs = (P("depth", "rows", "cols", None), P("depth", None, None, None, None))
    out_specs = (P("depth", "rows", "cols", None), P("depth", "rows", "cols", None))
    return jax.shard_map(
        on_device, mesh=mesh, in_specs=in_specs, out_specs=out_specs, check_vma=False
    )
```

```python
import functools

import jax
import jax.numpy as jnp
from jax import lax
from jax.experimental import pallas as pl
from jax.experimental.pallas import tpu as pltpu
from jax.sharding import PartitionSpec as P

AXES = ("depth", "rows", "cols")
BF16 = jnp.bfloat16
F32 = jnp.float32
KEPT = 2
SLOTS = {"prev": -1, "own": 0, "core": 1, "next": 2}
JUMP_HALO = {"prev": 4, "own": 3, "core": 2, "next": 0}


CHUNK = 2


def fill_row(patch, row, x, valid, inside=None):
    width, channels = x.shape
    act = x / (1.0 + jnp.exp(-x))
    act = jnp.where(valid, act, 0.0)
    if inside is not None:
        act = jnp.where(inside, act, 0.0)
    left = pltpu.roll(act, 1, 0)
    right = pltpu.roll(act, width - 1, 0)
    if inside is None:
        column = lax.broadcasted_iota(jnp.int32, (width, channels), 0)
        left = jnp.where(column == 0, 0.0, left)
        right = jnp.where(column == width - 1, 0.0, right)
    for tap, moved in enumerate((left, act, right)):
        patch[row, :, tap * channels : (tap + 1) * channels] = moved.astype(BF16)


def fill(patch, state, rows, first, height, inside=None):
    def body(row, carry):
        fill_row(patch, row, state[row], (first + row >= 0) & (first + row < height), inside)
        return carry

    lax.fori_loop(0, rows, body, 0, unroll=2)


def slopes(patch, weight, first, rows, emit, chunk=CHUNK):
    width, deep = patch.shape[1:]
    for start in range(first, first + rows, chunk):
        count = min(chunk, first + rows - start)
        total = None
        for tap in range(3):
            part = jnp.dot(
                patch[start + tap - 1 : start + tap - 1 + count].reshape(count * width, deep),
                weight[tap],
                preferred_element_type=F32,
            )
            total = part if total is None else total + part
        total = total.reshape(count, width, -1)
        for k in range(count):
            emit(start + k, total[k])


def strip_row(rows):
    return (lax.axis_index("rows") * lax.axis_size("cols") + lax.axis_index("cols")) * rows


def edge_kernel(pieces, low, high):
    rows, count = pieces.shape[1], low.shape[1]
    low[...] = pieces[:, :count].astype(BF16)
    high[...] = pieces[:, rows - count :].astype(BF16)


def head_kernel(step, height, pieces, above, below, layers, main, top, bottom, *rest):
    jumps, (state, first, patch, second) = rest[:-4], rest[-4:]
    ncols, rows, wide = pieces.shape[:3]
    halo = above.shape[1]
    deep = rows + 2 * halo
    origin = strip_row(rows) - halo
    for k in range(ncols):
        cut = slice(k * wide, (k + 1) * wide)
        state[:halo, cut] = above[k].astype(F32)
        state[halo : halo + rows, cut] = pieces[k]
        state[halo + rows :, cut] = below[k].astype(F32)
    main[...] = state[halo : halo + rows]
    top[...] = state[halo - top.shape[0] : halo].astype(BF16)
    bottom[...] = state[halo + rows : halo + rows + bottom.shape[0]].astype(BF16)
    fill(patch, state, deep, origin, height)

    def to_middle(row, slope):
        first[row] = slope
        valid = (origin + row >= 0) & (origin + row < height)
        fill_row(second, row, state[row] + step * slope, valid)

    def to_jump(row, slope):
        jump = step * (slope - first[row])
        for ref in jumps:
            place = row - (deep - ref.shape[0]) // 2
            if 0 <= place < ref.shape[0]:
                ref[place] = jump.astype(ref.dtype)

    slopes(patch, layers.at[0], 1, deep - 2, to_middle)
    slopes(second, layers.at[1], 2, deep - 4, to_jump)


def turn_kernel(host, rows, count, kept, given, last, step, height, *rest):
    outs = 0 if last else 4
    begin = len(rest) - (2 * count + given + outs + kept + 3)
    start, rest = rest[:begin], rest[begin:]
    weights, jumps = rest[:count], rest[count : 2 * count]
    weights = [weight.at[0] if len(weight.shape) == 4 else weight for weight in weights]
    rest = rest[2 * count + given :]
    if not last:
        out, out_top, out_bottom, left = rest[:4]
        rest = rest[4:]
    saved, (state, *patches) = rest[:kept], rest[kept:]

    @pl.when(lax.axis_index("depth") == host)
    def _():
        halo = (state.shape[0] - rows) // 2
        origin = strip_row(rows) - halo
        if len(start) == 1:
            state[...] = start[0][...]
        else:
            main, top, bottom = start
            state[:halo] = top[...].astype(F32)
            state[halo : halo + rows] = main[...].astype(F32)
            state[halo + rows :] = bottom[...].astype(F32)
        if kept:
            saved[0][...] = state[halo - KEPT : halo + rows + KEPT]
        fill(patches[0], state, rows + 2 * halo, origin, height)
        for k in range(count):
            ends = k == count - 1
            far = 0 if ends and not last else halo - k - 1
            cut = halo - (jumps[k].shape[0] - rows) // 2

            def advance(row, slope):
                new = state[row] + (2.0 * step) * slope + jumps[k][row - cut].astype(F32)
                if k < kept - 1 and halo - KEPT <= row < halo + rows + KEPT:
                    saved[k + 1][row - halo + KEPT] = new
                if not ends:
                    state[row] = new
                    fill_row(patches[(k + 1) % 2], row, new, (origin + row >= 0) & (origin + row < height))
                elif not last:
                    place, edge = row - halo, out_top.shape[0]
                    high = new.astype(BF16)
                    out[place] = high
                    left[place] = (new - high.astype(F32)).astype(left.dtype)
                    if place < edge:
                        out_top[place] = high
                    if place >= rows - edge:
                        out_bottom[place - rows + edge] = high

            slopes(patches[k % 2], weights[k], halo - far, rows + 2 * far, advance)


def settle_kernel(host, sends, low, *rest):
    if sends:
        left, rest = rest[0], rest[1:]
    kept = len(rest) // 2 if not sends else (len(rest) - 1) // 2
    given, outs = rest[:kept], rest[kept:]

    @pl.when(lax.axis_index("depth") == host)
    def _():
        rows = low.shape[0]
        part = low[...].astype(F32)
        if sends:
            outs[0][...] = (left[...] + part).astype(BF16)
        for old, new in zip(given, outs[1:] if sends else outs):
            new[KEPT : KEPT + rows] = old[KEPT : KEPT + rows] + part


def pack_kernel(own, core, after, prev, packed, state):
    depth = lax.axis_index("depth")
    final = 4 * ((lax.axis_size("depth") - 1) // 4) + 2
    role = jnp.where(depth < final, depth % 4, depth - final)
    for k, source in enumerate((own, core, after, prev)):

        @pl.when(role == k)
        def _():
            state[...] = source[...]

    ncols = packed.shape[0]
    deep, width, channels = state.shape
    wide = width // ncols
    rows = deep - 2 * KEPT
    first = lax.axis_index("cols") == 0
    group = lax.broadcasted_iota(jnp.int32, (8, channels), 0)
    span = wide + 8
    for k in range(ncols):
        for row in range(rows + KEPT):
            if row < rows:
                line = lambda a, b: state[KEPT + row, a:b]
            else:
                line = lambda a, b: jnp.where(first, state[row - rows, a:b], state[KEPT + row, a:b])
            mine = line(k * wide, (k + 1) * wide)
            right = line((k + 1) * wide, (k + 1) * wide + 8) if k < ncols - 1 else jnp.zeros((8, channels), F32)
            left = line(k * wide - 8, k * wide) if k > 0 else jnp.zeros((8, channels), F32)
            high = mine.astype(BF16)
            packed[k, row * span : row * span + wide] = high
            packed[k, row * span + wide : (row + 1) * span] = jnp.where(group < 4, right, left).astype(BF16)
            if row < rows:
                start = (rows + KEPT) * span + row * wide
                packed[k, start : start + wide] = (mine - high.astype(F32)).astype(BF16)


def tail_kernel(step, height, width, packed, layers, fine, coarse, state, patch, second):
    ncols = packed.shape[0]
    tile_rows, wide = coarse.shape[:2]
    rows = tile_rows // ncols
    span = wide + 8
    for k in range(ncols):
        for row in range(rows):
            start = (rows + KEPT) * span + row * wide
            high = packed[k, row * span : (row + 1) * span].astype(F32)
            whole = high[:wide] + packed[k, start : start + wide].astype(F32)
            place = k * rows + row
            coarse[place] = whole
            state[KEPT + place, :wide] = whole
            state[KEPT + place, wide:] = high[wide:]
    for row in range(KEPT):
        cut = slice((rows + row) * span, (rows + row + 1) * span)
        state[row] = packed[0, cut].astype(F32)
        state[KEPT + tile_rows + row] = packed[ncols - 1, cut].astype(F32)
    top = lax.axis_index("rows") * tile_rows - KEPT
    column = lax.broadcasted_iota(jnp.int32, (span, state.shape[2]), 0)
    place = lax.axis_index("cols") * wide + jnp.where(column < span - 4, column, column - span)
    inside = (place >= 0) & (place < width)
    fill(patch, state, tile_rows + 2 * KEPT, top, height, inside)

    def to_middle(row, slope):
        middle = state[row] + step * slope
        if KEPT <= row < KEPT + tile_rows:
            fine[0, row - KEPT] = middle[:wide]
        fill_row(second, row, middle, (top + row >= 0) & (top + row < height), inside)

    def to_ending(row, slope):
        fine[1, row - KEPT] = fine[0, row - KEPT] + step * slope[:wide]

    slopes(patch, layers.at[0], 1, tile_rows + 2, to_middle, 2 * CHUNK)
    slopes(second, layers.at[1], 2, tile_rows, to_ending, 2 * CHUNK)


def call(kernel, outs, scratch, inputs, aliases={}, vmem=12 << 20, work=0):
    return pl.pallas_call(
        kernel,
        out_shape=[jax.ShapeDtypeStruct(*o) for o in outs],
        in_specs=[pl.BlockSpec(memory_space=pltpu.VMEM)] * len(inputs),
        out_specs=[pl.BlockSpec(memory_space=pltpu.VMEM)] * len(outs),
        scratch_shapes=scratch,
        input_output_aliases=aliases,
        compiler_params=pltpu.CompilerParams(vmem_limit_bytes=vmem),
        cost_estimate=pl.CostEstimate(flops=work, bytes_accessed=0, transcendentals=0) if work else None,
    )(*inputs)


def on_device(section_states, weights):
    ndepth, nrows, ncols = (lax.axis_size(a) for a in AXES)
    tile = section_states[0]
    tile_rows, tile_cols, channels = tile.shape
    height, width = tile_rows * nrows, tile_cols * ncols
    rows = tile_rows // ncols
    strips = nrows * ncols
    step = 2.0 / (2 * ndepth)
    flat = weights.reshape(2, 3, 3 * channels, channels)
    w0 = flat[0]

    hosts = [*range(0, ndepth, 4), ndepth - 2]
    visits = [["own", "core", "next"]] + [["prev", "own", "core", "next"]] * (len(hosts) - 2) + [["own"]]
    visits[-2] = ["prev", "own", "core"]
    halos = [len(v) + 1 for v in visits]
    halos[-1] += 1

    def route(pairs, shift):
        return [
            (a * strips + s, b * strips + (s + shift))
            for a, b in pairs
            for s in range(strips)
            if 0 <= s + shift < strips
        ]

    def fetch(x, slot, only=hosts):
        away = SLOTS[slot]
        pairs = [(h + away, h) for h, v in zip(hosts, visits) if slot in v and h in only]
        return lax.ppermute(x, AXES, route(pairs, 0))

    def ring(x, shift):
        return lax.ppermute(x, ("rows", "cols"), [(s, (s + shift) % strips) for s in range(strips)])

    far = ("next", "core", "prev")
    all_weights = {"own": flat} | {slot: fetch(w0, slot) for slot in far}

    pieces = lax.all_to_all(tile.reshape(ncols, rows, tile_cols, channels), "cols", 0, 0, tiled=True)
    near = JUMP_HALO["prev"] + 2
    low, high = call(edge_kernel, [((ncols, near, tile_cols, channels), BF16)] * 2, [], (pieces,))
    above, below = ring(high, 1), ring(low, -1)
    above, below, all_weights["next"] = lax.optimization_barrier((above, below, all_weights["next"]))
    like = lambda n, t=F32: ((n, width, channels), t)
    vm = lambda n: pltpu.VMEM((n, width, channels), F32)
    patch = lambda n: pltpu.VMEM((n, width, 3 * channels), BF16)
    deep = rows + 2 * near
    kinds = {"prev": BF16, "own": F32, "core": F32, "next": BF16}
    main, top, bottom, *jumps = call(
        functools.partial(head_kernel, step, height),
        [like(rows), like(halos[0], BF16), like(halos[0], BF16)]
        + [like(rows + 2 * JUMP_HALO[slot], kinds[slot]) for slot in SLOTS],
        [vm(deep), vm(deep), patch(deep), patch(deep)],
        (pieces, above, below, flat),
        work=15_000_000_000,
    )
    *jumps, all_weights["core"] = lax.optimization_barrier((*jumps, all_weights["core"]))
    all_jumps = dict(zip(SLOTS, jumps))
    first_jump = fetch(all_jumps["next"], "next", hosts[:1])
    all_jumps |= {slot: fetch(all_jumps[slot], slot, hosts[1:] if slot == "next" else hosts) for slot in far}

    saved = {}
    start = (main, top, bottom)
    turns = list(zip(hosts, visits, halos))
    turns[:1] = [(hosts[0], visits[0][:-1], halos[0]), (hosts[0], visits[0][-1:], KEPT)]
    for turn, (host, visit, halo) in enumerate(turns):
        last = turn in (0, len(turns) - 1)
        keeps = [] if turn == 1 else [*visit, "next" if turn == 0 else "core"] if last else visit
        given = [slot for slot in keeps if slot in saved]
        left = like(rows, BF16 if turn == 1 else F32)
        outs = [] if last else [like(rows, BF16)] + [like(turns[turn + 1][2], BF16)] * 2 + [left]
        inputs = (
            *start,
            *(all_weights[slot] for slot in visit),
            *(first_jump if turn == 1 else all_jumps[slot] for slot in visit),
            *(saved[slot] for slot in given),
        )
        results = call(
            functools.partial(turn_kernel, host, rows, len(visit), len(keeps), len(given), last, step, height),
            outs + [like(rows + 2 * KEPT)] * len(keeps),
            [vm(rows + 2 * halo), patch(rows + 2 * halo), patch(rows + 2 * halo)],
            inputs,
            {len(inputs) - len(given) + k: len(outs) + keeps.index(slot) for k, slot in enumerate(given)},
            work=20_000_000_000 if turn > 1 else 0,
        )
        saved |= zip(keeps, results[len(outs) :])
        if turn == 0:
            start = (saved["next"],)
            continue
        if turn > 1:
            inputs = (low, *(() if last else results[3:4]), *(saved[slot] for slot in keeps))
            settled = call(
                functools.partial(settle_kernel, host, not last),
                ([] if last else [like(rows, BF16)]) + [like(rows + 2 * KEPT)] * len(keeps),
                [],
                inputs,
                {len(inputs) - len(keeps) + k: int(not last) + k for k in range(len(keeps))},
                work=20_000_000_000,
            )
            saved |= zip(keeps, settled[int(not last) :])
        if not last:
            pair = [(host, turns[turn + 1][0])]
            main = lax.ppermute(results[0], AXES, route(pair, 0))
            top = lax.ppermute(results[2], AXES, route(pair, 1))
            bottom = lax.ppermute(results[1], AXES, route(pair, -1))
            low = lax.ppermute(results[3] if turn == 1 else settled[0], AXES, route(pair, 0))
            start = (main, top, bottom)

    visits[-1] = ["own", "core"]

    def give(slot):
        away = SLOTS[slot]
        return lax.ppermute(saved[slot], AXES, route([(h, h + away) for h, v in zip(hosts, visits) if slot in v], 0))

    span = tile_cols + 8
    pixels = (rows + KEPT) * span + rows * tile_cols
    (packed,) = call(
        pack_kernel,
        [((ncols, pixels, channels), BF16)],
        [vm(rows + 2 * KEPT)],
        (saved["own"], give("core"), give("next"), give("prev")),
    )
    packed = lax.all_to_all(packed, "cols", 0, 0, tiled=True)
    tall = lambda n, t=F32, taps=1: pltpu.VMEM((n, span, taps * channels), t)
    fine, coarse = call(
        functools.partial(tail_kernel, step, height, width),
        [((2, *tile.shape), F32), (tile.shape, F32)],
        [tall(tile_rows + 4), tall(tile_rows + 4, BF16, 3), tall(tile_rows + 4, BF16, 3)],
        (packed, flat),
    )
    return fine, coarse[None]


def solution(mesh):
    in_specs = (P("depth", "rows", "cols", None), P("depth", None, None, None, None))
    out_specs = (P("depth", "rows", "cols", None), P("depth", "rows", "cols", None))
    return jax.shard_map(
        on_device, mesh=mesh, in_specs=in_specs, out_specs=out_specs, check_vma=False
    )
```

```python
import functools

import jax
import jax.numpy as jnp
from jax import lax
from jax.experimental import pallas as pl
from jax.experimental.pallas import tpu as pltpu
from jax.sharding import PartitionSpec as P

AXES = ("depth", "rows", "cols")
BF16 = jnp.bfloat16
F32 = jnp.float32
KEPT = 2
SLOTS = {"prev": -1, "own": 0, "core": 1, "next": 2}
JUMP_HALO = {"prev": 4, "own": 3, "core": 2, "next": 0}


CHUNK = 2


def fill_row(patch, row, x, valid, inside=None):
    width, channels = x.shape
    act = x / (1.0 + jnp.exp(-x))
    act = jnp.where(valid, act, 0.0)
    if inside is not None:
        act = jnp.where(inside, act, 0.0)
    left = pltpu.roll(act, 1, 0)
    right = pltpu.roll(act, width - 1, 0)
    if inside is None:
        column = lax.broadcasted_iota(jnp.int32, (width, channels), 0)
        left = jnp.where(column == 0, 0.0, left)
        right = jnp.where(column == width - 1, 0.0, right)
    for tap, moved in enumerate((left, act, right)):
        patch[row, :, tap * channels : (tap + 1) * channels] = moved.astype(BF16)


def fill(patch, state, rows, first, height, inside=None):
    def body(row, carry):
        fill_row(patch, row, state[row], (first + row >= 0) & (first + row < height), inside)
        return carry

    lax.fori_loop(0, rows, body, 0, unroll=2)


def slopes(patch, weight, first, rows, emit, chunk=CHUNK):
    width, deep = patch.shape[1:]
    for start in range(first, first + rows, chunk):
        count = min(chunk, first + rows - start)
        total = None
        for tap in range(3):
            part = jnp.dot(
                patch[start + tap - 1 : start + tap - 1 + count].reshape(count * width, deep),
                weight[tap],
                preferred_element_type=F32,
            )
            total = part if total is None else total + part
        total = total.reshape(count, width, -1)
        for k in range(count):
            emit(start + k, total[k])


def strip_row(rows):
    return (lax.axis_index("rows") * lax.axis_size("cols") + lax.axis_index("cols")) * rows


def edge_kernel(pieces, low, high):
    rows, count = pieces.shape[1], low.shape[1]
    low[...] = pieces[:, :count].astype(BF16)
    high[...] = pieces[:, rows - count :].astype(BF16)


def head_kernel(step, height, pieces, above, below, layers, main, top, bottom, *rest):
    jumps, (state, first, patch, second) = rest[:-4], rest[-4:]
    ncols, rows, wide = pieces.shape[:3]
    halo = above.shape[1]
    deep = rows + 2 * halo
    origin = strip_row(rows) - halo
    for k in range(ncols):
        cut = slice(k * wide, (k + 1) * wide)
        state[:halo, cut] = above[k].astype(F32)
        state[halo : halo + rows, cut] = pieces[k]
        state[halo + rows :, cut] = below[k].astype(F32)
    main[...] = state[halo : halo + rows]
    top[...] = state[halo - top.shape[0] : halo].astype(BF16)
    bottom[...] = state[halo + rows : halo + rows + bottom.shape[0]].astype(BF16)
    fill(patch, state, deep, origin, height)

    def to_middle(row, slope):
        first[row] = slope
        valid = (origin + row >= 0) & (origin + row < height)
        fill_row(second, row, state[row] + step * slope, valid)

    def to_jump(row, slope):
        jump = step * (slope - first[row])
        for ref in jumps:
            place = row - (deep - ref.shape[0]) // 2
            if 0 <= place < ref.shape[0]:
                ref[place] = jump.astype(ref.dtype)

    slopes(patch, layers.at[0], 1, deep - 2, to_middle)
    slopes(second, layers.at[1], 2, deep - 4, to_jump)


def turn_kernel(host, rows, count, kept, given, last, step, height, *rest):
    outs = 0 if last else 4
    begin = len(rest) - (2 * count + given + outs + kept + 3)
    start, rest = rest[:begin], rest[begin:]
    weights, jumps = rest[:count], rest[count : 2 * count]
    weights = [weight.at[0] if len(weight.shape) == 4 else weight for weight in weights]
    rest = rest[2 * count + given :]
    if not last:
        out, out_top, out_bottom, left = rest[:4]
        rest = rest[4:]
    saved, (state, *patches) = rest[:kept], rest[kept:]

    @pl.when(lax.axis_index("depth") == host)
    def _():
        halo = (state.shape[0] - rows) // 2
        origin = strip_row(rows) - halo
        if len(start) == 1:
            state[...] = start[0][...]
        else:
            main, top, bottom = start
            state[:halo] = top[...].astype(F32)
            state[halo : halo + rows] = main[...].astype(F32)
            state[halo + rows :] = bottom[...].astype(F32)
        if kept:
            saved[0][...] = state[halo - KEPT : halo + rows + KEPT]
        fill(patches[0], state, rows + 2 * halo, origin, height)
        for k in range(count):
            ends = k == count - 1
            far = 0 if ends and not last else halo - k - 1
            cut = halo - (jumps[k].shape[0] - rows) // 2

            def advance(row, slope):
                new = state[row] + (2.0 * step) * slope + jumps[k][row - cut].astype(F32)
                if k < kept - 1 and halo - KEPT <= row < halo + rows + KEPT:
                    saved[k + 1][row - halo + KEPT] = new
                if not ends:
                    state[row] = new
                    fill_row(patches[(k + 1) % 2], row, new, (origin + row >= 0) & (origin + row < height))
                elif not last:
                    place, edge = row - halo, out_top.shape[0]
                    high = new.astype(BF16)
                    out[place] = high
                    left[place] = (new - high.astype(F32)).astype(left.dtype)
                    if place < edge:
                        out_top[place] = high
                    if place >= rows - edge:
                        out_bottom[place - rows + edge] = high

            slopes(patches[k % 2], weights[k], halo - far, rows + 2 * far, advance)


def settle_kernel(host, sends, low, *rest):
    if sends:
        left, rest = rest[0], rest[1:]
    kept = len(rest) // 2 if not sends else (len(rest) - 1) // 2
    given, outs = rest[:kept], rest[kept:]

    @pl.when(lax.axis_index("depth") == host)
    def _():
        rows = low.shape[0]
        part = low[...].astype(F32)
        if sends:
            outs[0][...] = (left[...] + part).astype(BF16)
        for old, new in zip(given, outs[1:] if sends else outs):
            new[KEPT : KEPT + rows] = old[KEPT : KEPT + rows] + part


def pack_kernel(own, core, after, prev, packed, state):
    depth = lax.axis_index("depth")
    final = 4 * ((lax.axis_size("depth") - 1) // 4) + 2
    role = jnp.where(depth < final, depth % 4, depth - final)
    for k, source in enumerate((own, core, after, prev)):

        @pl.when(role == k)
        def _():
            state[...] = source[...]

    ncols = packed.shape[0]
    deep, width, channels = state.shape
    wide = width // ncols
    rows = deep - 2 * KEPT
    first = lax.axis_index("cols") == 0
    group = lax.broadcasted_iota(jnp.int32, (8, channels), 0)
    span = wide + 8
    for k in range(ncols):
        for row in range(rows + KEPT):
            if row < rows:
                line = lambda a, b: state[KEPT + row, a:b]
            else:
                line = lambda a, b: jnp.where(first, state[row - rows, a:b], state[KEPT + row, a:b])
            mine = line(k * wide, (k + 1) * wide)
            right = line((k + 1) * wide, (k + 1) * wide + 8) if k < ncols - 1 else jnp.zeros((8, channels), F32)
            left = line(k * wide - 8, k * wide) if k > 0 else jnp.zeros((8, channels), F32)
            high = mine.astype(BF16)
            packed[k, row * span : row * span + wide] = high
            packed[k, row * span + wide : (row + 1) * span] = jnp.where(group < 4, right, left).astype(BF16)
            if row < rows:
                start = (rows + KEPT) * span + row * wide
                packed[k, start : start + wide] = (mine - high.astype(F32)).astype(BF16)


def tail_kernel(step, height, width, packed, layers, fine, coarse, state, patch, second):
    ncols = packed.shape[0]
    tile_rows, wide = coarse.shape[:2]
    rows = tile_rows // ncols
    span = wide + 8
    for k in range(ncols):
        for row in range(rows):
            start = (rows + KEPT) * span + row * wide
            high = packed[k, row * span : (row + 1) * span].astype(F32)
            whole = high[:wide] + packed[k, start : start + wide].astype(F32)
            place = k * rows + row
            coarse[place] = whole
            state[KEPT + place, :wide] = whole
            state[KEPT + place, wide:] = high[wide:]
    for row in range(KEPT):
        cut = slice((rows + row) * span, (rows + row + 1) * span)
        state[row] = packed[0, cut].astype(F32)
        state[KEPT + tile_rows + row] = packed[ncols - 1, cut].astype(F32)
    top = lax.axis_index("rows") * tile_rows - KEPT
    column = lax.broadcasted_iota(jnp.int32, (span, state.shape[2]), 0)
    place = lax.axis_index("cols") * wide + jnp.where(column < span - 4, column, column - span)
    inside = (place >= 0) & (place < width)
    fill(patch, state, tile_rows + 2 * KEPT, top, height, inside)

    def to_middle(row, slope):
        middle = state[row] + step * slope
        if KEPT <= row < KEPT + tile_rows:
            fine[0, row - KEPT] = middle[:wide]
        fill_row(second, row, middle, (top + row >= 0) & (top + row < height), inside)

    def to_ending(row, slope):
        fine[1, row - KEPT] = fine[0, row - KEPT] + step * slope[:wide]

    slopes(patch, layers.at[0], 1, tile_rows + 2, to_middle, 2 * CHUNK)
    slopes(second, layers.at[1], 2, tile_rows, to_ending, 2 * CHUNK)


def call(kernel, outs, scratch, inputs, aliases={}, vmem=12 << 20, work=0):
    return pl.pallas_call(
        kernel,
        out_shape=[jax.ShapeDtypeStruct(*o) for o in outs],
        in_specs=[pl.BlockSpec(memory_space=pltpu.VMEM)] * len(inputs),
        out_specs=[pl.BlockSpec(memory_space=pltpu.VMEM)] * len(outs),
        scratch_shapes=scratch,
        input_output_aliases=aliases,
        compiler_params=pltpu.CompilerParams(vmem_limit_bytes=vmem),
        cost_estimate=pl.CostEstimate(flops=work, bytes_accessed=0, transcendentals=0) if work else None,
    )(*inputs)


def on_device(section_states, weights):
    ndepth, nrows, ncols = (lax.axis_size(a) for a in AXES)
    tile = section_states[0]
    tile_rows, tile_cols, channels = tile.shape
    height, width = tile_rows * nrows, tile_cols * ncols
    rows = tile_rows // ncols
    strips = nrows * ncols
    step = 2.0 / (2 * ndepth)
    flat = weights.reshape(2, 3, 3 * channels, channels)
    w0 = flat[0]

    hosts = [*range(0, ndepth, 4), ndepth - 2]
    visits = [["own", "core", "next"]] + [["prev", "own", "core", "next"]] * (len(hosts) - 2) + [["own"]]
    visits[-2] = ["prev", "own", "core"]
    halos = [len(v) + 1 for v in visits]
    halos[-1] += 1

    def route(pairs, shift):
        return [
            (a * strips + s, b * strips + (s + shift))
            for a, b in pairs
            for s in range(strips)
            if 0 <= s + shift < strips
        ]

    def fetch(x, slot, only=hosts):
        away = SLOTS[slot]
        pairs = [(h + away, h) for h, v in zip(hosts, visits) if slot in v and h in only]
        return lax.ppermute(x, AXES, route(pairs, 0))

    def ring(x, shift):
        return lax.ppermute(x, ("rows", "cols"), [(s, (s + shift) % strips) for s in range(strips)])

    far = ("next", "core", "prev")
    all_weights = {"own": flat} | {slot: fetch(w0, slot) for slot in far}

    pieces = lax.all_to_all(tile.reshape(ncols, rows, tile_cols, channels), "cols", 0, 0, tiled=True)
    near = JUMP_HALO["prev"] + 2
    low, high = call(edge_kernel, [((ncols, near, tile_cols, channels), BF16)] * 2, [], (pieces,))
    above, below = ring(high, 1), ring(low, -1)
    early = [all_weights[slot] for slot in ("next", "prev")]
    above, below, all_weights["next"], all_weights["prev"] = lax.optimization_barrier((above, below, *early))
    like = lambda n, t=F32: ((n, width, channels), t)
    vm = lambda n: pltpu.VMEM((n, width, channels), F32)
    patch = lambda n: pltpu.VMEM((n, width, 3 * channels), BF16)
    deep = rows + 2 * near
    kinds = {"prev": BF16, "own": F32, "core": F32, "next": BF16}
    main, top, bottom, *jumps = call(
        functools.partial(head_kernel, step, height),
        [like(rows), like(halos[0], BF16), like(halos[0], BF16)]
        + [like(rows + 2 * JUMP_HALO[slot], kinds[slot]) for slot in SLOTS],
        [vm(deep), vm(deep), patch(deep), patch(deep)],
        (pieces, above, below, flat),
        work=15_000_000_000,
    )
    *jumps, all_weights["core"] = lax.optimization_barrier((*jumps, all_weights["core"]))
    all_jumps = dict(zip(SLOTS, jumps))
    first_jump = fetch(all_jumps["next"], "next", hosts[:1])
    all_jumps |= {slot: fetch(all_jumps[slot], slot, hosts[1:] if slot == "next" else hosts) for slot in far}

    saved = {}
    start = (main, top, bottom)
    turns = list(zip(hosts, visits, halos))
    turns[:1] = [(hosts[0], visits[0][:-1], halos[0]), (hosts[0], visits[0][-1:], KEPT)]
    for turn, (host, visit, halo) in enumerate(turns):
        last = turn in (0, len(turns) - 1)
        keeps = [] if turn == 1 else [*visit, "next" if turn == 0 else "core"] if last else visit
        given = [slot for slot in keeps if slot in saved]
        left = like(rows, BF16 if turn == 1 else F32)
        outs = [] if last else [like(rows, BF16)] + [like(turns[turn + 1][2], BF16)] * 2 + [left]
        inputs = (
            *start,
            *(all_weights[slot] for slot in visit),
            *(first_jump if turn == 1 else all_jumps[slot] for slot in visit),
            *(saved[slot] for slot in given),
        )
        results = call(
            functools.partial(turn_kernel, host, rows, len(visit), len(keeps), len(given), last, step, height),
            outs + [like(rows + 2 * KEPT)] * len(keeps),
            [vm(rows + 2 * halo), patch(rows + 2 * halo), patch(rows + 2 * halo)],
            inputs,
            {len(inputs) - len(given) + k: len(outs) + keeps.index(slot) for k, slot in enumerate(given)},
            work=20_000_000_000 if turn > 1 else 0,
        )
        saved |= zip(keeps, results[len(outs) :])
        if turn == 0:
            start = (saved["next"],)
            continue
        if turn > 1:
            inputs = (low, *(() if last else results[3:4]), *(saved[slot] for slot in keeps))
            settled = call(
                functools.partial(settle_kernel, host, not last),
                ([] if last else [like(rows, BF16)]) + [like(rows + 2 * KEPT)] * len(keeps),
                [],
                inputs,
                {len(inputs) - len(keeps) + k: int(not last) + k for k in range(len(keeps))},
                work=20_000_000_000,
            )
            saved |= zip(keeps, settled[int(not last) :])
        if not last:
            pair = [(host, turns[turn + 1][0])]
            main = lax.ppermute(results[0], AXES, route(pair, 0))
            top = lax.ppermute(results[2], AXES, route(pair, 1))
            bottom = lax.ppermute(results[1], AXES, route(pair, -1))
            low = lax.ppermute(results[3] if turn == 1 else settled[0], AXES, route(pair, 0))
            start = (main, top, bottom)

    visits[-1] = ["own", "core"]

    def give(slot):
        away = SLOTS[slot]
        return lax.ppermute(saved[slot], AXES, route([(h, h + away) for h, v in zip(hosts, visits) if slot in v], 0))

    span = tile_cols + 8
    pixels = (rows + KEPT) * span + rows * tile_cols
    (packed,) = call(
        pack_kernel,
        [((ncols, pixels, channels), BF16)],
        [vm(rows + 2 * KEPT)],
        (saved["own"], give("core"), give("next"), give("prev")),
    )
    packed = lax.all_to_all(packed, "cols", 0, 0, tiled=True)
    tall = lambda n, t=F32, taps=1: pltpu.VMEM((n, span, taps * channels), t)
    fine, coarse = call(
        functools.partial(tail_kernel, step, height, width),
        [((2, *tile.shape), F32), (tile.shape, F32)],
        [tall(tile_rows + 4), tall(tile_rows + 4, BF16, 3), tall(tile_rows + 4, BF16, 3)],
        (packed, flat),
    )
    return fine, coarse[None]


def solution(mesh):
    in_specs = (P("depth", "rows", "cols", None), P("depth", None, None, None, None))
    out_specs = (P("depth", "rows", "cols", None), P("depth", "rows", "cols", None))
    return jax.shard_map(
        on_device, mesh=mesh, in_specs=in_specs, out_specs=out_specs, check_vma=False
    )
```

```python
import functools

import jax
import jax.numpy as jnp
from jax import lax
from jax.experimental import pallas as pl
from jax.experimental.pallas import tpu as pltpu
from jax.sharding import PartitionSpec as P

AXES = ("depth", "rows", "cols")
BF16 = jnp.bfloat16
F32 = jnp.float32
KEPT = 2
SLOTS = {"prev": -1, "own": 0, "core": 1, "next": 2}
JUMP_HALO = {"prev": 4, "own": 3, "core": 2, "next": 0}


CHUNK = 2


def fill_row(patch, row, x, valid, inside=None):
    width, channels = x.shape
    act = x / (1.0 + jnp.exp(-x))
    act = jnp.where(valid, act, 0.0)
    if inside is not None:
        act = jnp.where(inside, act, 0.0)
    left = pltpu.roll(act, 1, 0)
    right = pltpu.roll(act, width - 1, 0)
    if inside is None:
        column = lax.broadcasted_iota(jnp.int32, (width, channels), 0)
        left = jnp.where(column == 0, 0.0, left)
        right = jnp.where(column == width - 1, 0.0, right)
    for tap, moved in enumerate((left, act, right)):
        patch[row, :, tap * channels : (tap + 1) * channels] = moved.astype(BF16)


def fill(patch, state, rows, first, height, inside=None):
    def body(row, carry):
        fill_row(patch, row, state[row], (first + row >= 0) & (first + row < height), inside)
        return carry

    lax.fori_loop(0, rows, body, 0, unroll=2)


def slopes(patch, weight, first, rows, emit, chunk=CHUNK):
    width, deep = patch.shape[1:]
    for start in range(first, first + rows, chunk):
        count = min(chunk, first + rows - start)
        total = None
        for tap in range(3):
            part = jnp.dot(
                patch[start + tap - 1 : start + tap - 1 + count].reshape(count * width, deep),
                weight[tap],
                preferred_element_type=F32,
            )
            total = part if total is None else total + part
        total = total.reshape(count, width, -1)
        for k in range(count):
            emit(start + k, total[k])


def strip_row(rows):
    return (lax.axis_index("rows") * lax.axis_size("cols") + lax.axis_index("cols")) * rows


def edge_kernel(pieces, low, high):
    rows, count = pieces.shape[1], low.shape[1]
    low[...] = pieces[:, :count].astype(BF16)
    high[...] = pieces[:, rows - count :].astype(BF16)


def head_kernel(step, height, pieces, above, below, layers, main, top, bottom, *rest):
    jumps, (state, first, patch, second) = rest[:-4], rest[-4:]
    ncols, rows, wide = pieces.shape[:3]
    halo = above.shape[1]
    deep = rows + 2 * halo
    origin = strip_row(rows) - halo
    for k in range(ncols):
        cut = slice(k * wide, (k + 1) * wide)
        state[:halo, cut] = above[k].astype(F32)
        state[halo : halo + rows, cut] = pieces[k]
        state[halo + rows :, cut] = below[k].astype(F32)
    main[...] = state[halo : halo + rows]
    top[...] = state[halo - top.shape[0] : halo].astype(BF16)
    bottom[...] = state[halo + rows : halo + rows + bottom.shape[0]].astype(BF16)
    fill(patch, state, deep, origin, height)

    def to_middle(row, slope):
        first[row] = slope
        valid = (origin + row >= 0) & (origin + row < height)
        fill_row(second, row, state[row] + step * slope, valid)

    def to_jump(row, slope):
        jump = step * (slope - first[row])
        for ref in jumps:
            place = row - (deep - ref.shape[0]) // 2
            if 0 <= place < ref.shape[0]:
                ref[place] = jump.astype(ref.dtype)

    slopes(patch, layers.at[0], 1, deep - 2, to_middle)
    slopes(second, layers.at[1], 2, deep - 4, to_jump)


def turn_kernel(host, rows, count, kept, given, last, step, height, *rest):
    outs = 0 if last else 4
    begin = len(rest) - (2 * count + given + outs + kept + 3)
    start, rest = rest[:begin], rest[begin:]
    weights, jumps = rest[:count], rest[count : 2 * count]
    weights = [weight.at[0] if len(weight.shape) == 4 else weight for weight in weights]
    rest = rest[2 * count + given :]
    if not last:
        out, out_top, out_bottom, left = rest[:4]
        rest = rest[4:]
    saved, (state, *patches) = rest[:kept], rest[kept:]

    @pl.when(lax.axis_index("depth") == host)
    def _():
        halo = (state.shape[0] - rows) // 2
        origin = strip_row(rows) - halo
        if len(start) == 1:
            state[...] = start[0][...]
        else:
            main, top, bottom = start
            state[:halo] = top[...].astype(F32)
            state[halo : halo + rows] = main[...].astype(F32)
            state[halo + rows :] = bottom[...].astype(F32)
        if kept:
            saved[0][...] = state[halo - KEPT : halo + rows + KEPT]
        fill(patches[0], state, rows + 2 * halo, origin, height)
        for k in range(count):
            ends = k == count - 1
            far = 0 if ends and not last else halo - k - 1
            cut = halo - (jumps[k].shape[0] - rows) // 2

            def advance(row, slope):
                new = state[row] + (2.0 * step) * slope + jumps[k][row - cut].astype(F32)
                if k < kept - 1 and halo - KEPT <= row < halo + rows + KEPT:
                    saved[k + 1][row - halo + KEPT] = new
                if not ends:
                    state[row] = new
                    fill_row(patches[(k + 1) % 2], row, new, (origin + row >= 0) & (origin + row < height))
                elif not last:
                    place, edge = row - halo, out_top.shape[0]
                    high = new.astype(BF16)
                    out[place] = high
                    left[place] = (new - high.astype(F32)).astype(left.dtype)
                    if place < edge:
                        out_top[place] = high
                    if place >= rows - edge:
                        out_bottom[place - rows + edge] = high

            slopes(patches[k % 2], weights[k], halo - far, rows + 2 * far, advance)


def settle_kernel(host, sends, low, *rest):
    if sends:
        left, rest = rest[0], rest[1:]
    kept = len(rest) // 2 if not sends else (len(rest) - 1) // 2
    given, outs = rest[:kept], rest[kept:]

    @pl.when(lax.axis_index("depth") == host)
    def _():
        rows = low.shape[0]
        part = low[...].astype(F32)
        if sends:
            outs[0][...] = (left[...] + part).astype(BF16)
        for old, new in zip(given, outs[1:] if sends else outs):
            new[KEPT : KEPT + rows] = old[KEPT : KEPT + rows] + part


def pack_kernel(own, core, after, prev, *rest):
    packs, state = rest[:-1], rest[-1]
    depth = lax.axis_index("depth")
    final = 4 * ((lax.axis_size("depth") - 1) // 4) + 2
    role = jnp.where(depth < final, depth % 4, depth - final)
    for k, source in enumerate((own, core, after, prev)):

        @pl.when(role == k)
        def _():
            state[...] = source[...]

    ncols = len(packs)
    deep, width, channels = state.shape
    wide = width // ncols
    rows = deep - 2 * KEPT
    mine = lax.axis_index("cols")
    group = lax.broadcasted_iota(jnp.int32, (8, channels), 0)
    span = wide + 8
    for away, packed in enumerate(packs):
        k = lax.rem(mine + away, ncols)
        middle = pl.multiple_of(k * wide, 8)
        before = pl.multiple_of(jnp.maximum(middle - 8, 0), 8)
        after_it = pl.multiple_of(jnp.minimum(middle + wide, width - 8), 8)
        for row in range(rows + KEPT):
            if row < rows:
                place = KEPT + row
            else:
                place = jnp.where(mine == 0, row - rows, KEPT + row)
            here = state[place, pl.ds(middle, wide)]
            right = jnp.where(k < ncols - 1, state[place, pl.ds(after_it, 8)], 0.0)
            left = jnp.where(k > 0, state[place, pl.ds(before, 8)], 0.0)
            high = here.astype(BF16)
            packed[row * span : row * span + wide] = high
            packed[row * span + wide : (row + 1) * span] = jnp.where(group < 4, right, left).astype(BF16)
            if row < rows:
                start = (rows + KEPT) * span + row * wide
                packed[start : start + wide] = (here - high.astype(F32)).astype(BF16)


def tail_kernel(step, height, width, *rest):
    *packs, layers, fine, coarse, state, patch, second = rest
    ncols = len(packs)
    tile_rows, wide = coarse.shape[:2]
    rows = tile_rows // ncols
    span = wide + 8
    for away, packed in enumerate(packs):
        k = lax.rem(lax.axis_index("cols") + ncols - away, ncols)
        for row in range(rows):
            start = (rows + KEPT) * span + row * wide
            high = packed[row * span : (row + 1) * span].astype(F32)
            whole = high[:wide] + packed[start : start + wide].astype(F32)
            place = k * rows + row
            coarse[place] = whole
            state[KEPT + place, :wide] = whole
            state[KEPT + place, wide:] = high[wide:]
        for end, first in ((0, 0), (ncols - 1, KEPT + tile_rows)):

            @pl.when(k == end)
            def _():
                for row in range(KEPT):
                    state[first + row] = packed[(rows + row) * span : (rows + row + 1) * span].astype(F32)

    top = lax.axis_index("rows") * tile_rows - KEPT
    column = lax.broadcasted_iota(jnp.int32, (span, state.shape[2]), 0)
    place = lax.axis_index("cols") * wide + jnp.where(column < span - 4, column, column - span)
    inside = (place >= 0) & (place < width)
    fill(patch, state, tile_rows + 2 * KEPT, top, height, inside)

    def to_middle(row, slope):
        middle = state[row] + step * slope
        if KEPT <= row < KEPT + tile_rows:
            fine[0, row - KEPT] = middle[:wide]
        fill_row(second, row, middle, (top + row >= 0) & (top + row < height), inside)

    def to_ending(row, slope):
        fine[1, row - KEPT] = fine[0, row - KEPT] + step * slope[:wide]

    slopes(patch, layers.at[0], 1, tile_rows + 2, to_middle, 2 * CHUNK)
    slopes(second, layers.at[1], 2, tile_rows, to_ending, 2 * CHUNK)


def call(kernel, outs, scratch, inputs, aliases={}, vmem=12 << 20, work=0):
    return pl.pallas_call(
        kernel,
        out_shape=[jax.ShapeDtypeStruct(*o) for o in outs],
        in_specs=[pl.BlockSpec(memory_space=pltpu.VMEM)] * len(inputs),
        out_specs=[pl.BlockSpec(memory_space=pltpu.VMEM)] * len(outs),
        scratch_shapes=scratch,
        input_output_aliases=aliases,
        compiler_params=pltpu.CompilerParams(vmem_limit_bytes=vmem),
        cost_estimate=pl.CostEstimate(flops=work, bytes_accessed=0, transcendentals=0) if work else None,
    )(*inputs)


def on_device(section_states, weights):
    ndepth, nrows, ncols = (lax.axis_size(a) for a in AXES)
    tile = section_states[0]
    tile_rows, tile_cols, channels = tile.shape
    height, width = tile_rows * nrows, tile_cols * ncols
    rows = tile_rows // ncols
    strips = nrows * ncols
    step = 2.0 / (2 * ndepth)
    flat = weights.reshape(2, 3, 3 * channels, channels)
    w0 = flat[0]

    hosts = [*range(0, ndepth, 4), ndepth - 2]
    visits = [["own", "core", "next"]] + [["prev", "own", "core", "next"]] * (len(hosts) - 2) + [["own"]]
    visits[-2] = ["prev", "own", "core"]
    halos = [len(v) + 1 for v in visits]
    halos[-1] += 1

    def route(pairs, shift):
        return [
            (a * strips + s, b * strips + (s + shift))
            for a, b in pairs
            for s in range(strips)
            if 0 <= s + shift < strips
        ]

    def fetch(x, slot, only=hosts):
        away = SLOTS[slot]
        pairs = [(h + away, h) for h, v in zip(hosts, visits) if slot in v and h in only]
        return lax.ppermute(x, AXES, route(pairs, 0))

    def ring(x, shift):
        return lax.ppermute(x, ("rows", "cols"), [(s, (s + shift) % strips) for s in range(strips)])

    far = ("next", "core", "prev")
    all_weights = {"own": flat} | {slot: fetch(w0, slot) for slot in far}

    pieces = lax.all_to_all(tile.reshape(ncols, rows, tile_cols, channels), "cols", 0, 0, tiled=True)
    near = JUMP_HALO["prev"] + 2
    low, high = call(edge_kernel, [((ncols, near, tile_cols, channels), BF16)] * 2, [], (pieces,))
    above, below = ring(high, 1), ring(low, -1)
    above, below, all_weights["next"] = lax.optimization_barrier((above, below, all_weights["next"]))
    like = lambda n, t=F32: ((n, width, channels), t)
    vm = lambda n: pltpu.VMEM((n, width, channels), F32)
    patch = lambda n: pltpu.VMEM((n, width, 3 * channels), BF16)
    deep = rows + 2 * near
    kinds = {"prev": BF16, "own": F32, "core": F32, "next": BF16}
    main, top, bottom, *jumps = call(
        functools.partial(head_kernel, step, height),
        [like(rows), like(halos[0], BF16), like(halos[0], BF16)]
        + [like(rows + 2 * JUMP_HALO[slot], kinds[slot]) for slot in SLOTS],
        [vm(deep), vm(deep), patch(deep), patch(deep)],
        (pieces, above, below, flat),
        work=15_000_000_000,
    )
    *jumps, all_weights["core"] = lax.optimization_barrier((*jumps, all_weights["core"]))
    all_jumps = dict(zip(SLOTS, jumps))
    first_jump = fetch(all_jumps["next"], "next", hosts[:1])
    all_jumps |= {slot: fetch(all_jumps[slot], slot, hosts[1:] if slot == "next" else hosts) for slot in far}

    saved = {}
    start = (main, top, bottom)
    turns = list(zip(hosts, visits, halos))
    turns[:1] = [(hosts[0], visits[0][:-1], halos[0]), (hosts[0], visits[0][-1:], KEPT)]
    for turn, (host, visit, halo) in enumerate(turns):
        last = turn in (0, len(turns) - 1)
        keeps = [] if turn == 1 else [*visit, "next" if turn == 0 else "core"] if last else visit
        given = [slot for slot in keeps if slot in saved]
        left = like(rows, BF16 if turn == 1 else F32)
        outs = [] if last else [like(rows, BF16)] + [like(turns[turn + 1][2], BF16)] * 2 + [left]
        inputs = (
            *start,
            *(all_weights[slot] for slot in visit),
            *(first_jump if turn == 1 else all_jumps[slot] for slot in visit),
            *(saved[slot] for slot in given),
        )
        results = call(
            functools.partial(turn_kernel, host, rows, len(visit), len(keeps), len(given), last, step, height),
            outs + [like(rows + 2 * KEPT)] * len(keeps),
            [vm(rows + 2 * halo), patch(rows + 2 * halo), patch(rows + 2 * halo)],
            inputs,
            {len(inputs) - len(given) + k: len(outs) + keeps.index(slot) for k, slot in enumerate(given)},
            work=20_000_000_000 if turn > 1 else 0,
        )
        saved |= zip(keeps, results[len(outs) :])
        if turn == 0:
            start = (saved["next"],)
            continue
        if turn > 1:
            inputs = (low, *(() if last else results[3:4]), *(saved[slot] for slot in keeps))
            settled = call(
                functools.partial(settle_kernel, host, not last),
                ([] if last else [like(rows, BF16)]) + [like(rows + 2 * KEPT)] * len(keeps),
                [],
                inputs,
                {len(inputs) - len(keeps) + k: int(not last) + k for k in range(len(keeps))},
                work=20_000_000_000,
            )
            saved |= zip(keeps, settled[int(not last) :])
        if not last:
            pair = [(host, turns[turn + 1][0])]
            main = lax.ppermute(results[0], AXES, route(pair, 0))
            top = lax.ppermute(results[2], AXES, route(pair, 1))
            bottom = lax.ppermute(results[1], AXES, route(pair, -1))
            low = lax.ppermute(results[3] if turn == 1 else settled[0], AXES, route(pair, 0))
            start = (main, top, bottom)

    visits[-1] = ["own", "core"]

    def give(slot):
        away = SLOTS[slot]
        return lax.ppermute(saved[slot], AXES, route([(h, h + away) for h, v in zip(hosts, visits) if slot in v], 0))

    span = tile_cols + 8
    pixels = (rows + KEPT) * span + rows * tile_cols
    packs = list(call(
        pack_kernel,
        [((pixels, channels), BF16)] * ncols,
        [vm(rows + 2 * KEPT)],
        (saved["own"], give("core"), give("next"), give("prev")),
    ))
    for away in (2, 1, 3):
        packs[away] = lax.ppermute(packs[away], "cols", [(c, (c + away) % ncols) for c in range(ncols)])
    tall = lambda n, t=F32, taps=1: pltpu.VMEM((n, span, taps * channels), t)
    fine, coarse = call(
        functools.partial(tail_kernel, step, height, width),
        [((2, *tile.shape), F32), (tile.shape, F32)],
        [tall(tile_rows + 4), tall(tile_rows + 4, BF16, 3), tall(tile_rows + 4, BF16, 3)],
        (*packs, flat),
    )
    return fine, coarse[None]


def solution(mesh):
    in_specs = (P("depth", "rows", "cols", None), P("depth", None, None, None, None))
    out_specs = (P("depth", "rows", "cols", None), P("depth", "rows", "cols", None))
    return jax.shard_map(
        on_device, mesh=mesh, in_specs=in_specs, out_specs=out_specs, check_vma=False
    )
```
